32 devices in a mesh: depth: 4 (over y, x), col: 8 (over z, core).
Axes of the slice: x: 2, y: 2, z: 4, core: 2. Of those that a mesh axis runs over, the one named last changes fastest.
Arguments:
- raw_views: bfloat16 [8, 32, 8, 1024], P('depth', None, None, 'col'), may hold values from -48 to 48
- feat_weight: bfloat16 [9, 32, 32], replicated, may hold values from -0.375 to 0.375
- shifts: int32 [8, 96], replicated, may hold values from 0 to 127, as said below
- frame_range: int32 [8, 2], replicated, may hold values from 0 to 1024, as said below
- cost_weight: bfloat16 [27, 8, 32], replicated, may hold values from -0.21875 to 0.21875
- mid_weight: bfloat16 [27, 8, 8], replicated, may hold values from -0.4375 to 0.4375
- final_weight: bfloat16 [27, 8], replicated, may hold values from -17 to 17
Outputs:
- estimate: float32 [8, 1024], P(None, 'col')
The draws below stay inside these ranges and needn't reach their ends.
Inputs may be any that keep to these rules, and one draw needn't show every extreme that they name: `shifts`: shifts of view 0 are all zero; the largest shift is exactly 127. `frame_range`: row v holds the first and one past the last valid column of view v, the first below the second; view 0 is valid over all 1024 columns.
All inputs are finite; a program needn't handle non-finite values.
Results may differ from the reference program's by a relative error of at most 0.007.
The reference program's roundings to bfloat16 on the way (of `features`, `volume`, `first_act` and `second_act`) count: a program that leaves them out, or rounds other values in their place, can miss the bound.
Values may be sent and summed in bfloat16 or wider, within the bound.
A program may use at most 64 MiB of HBM per device.

```python
import math
import jax
import jax.numpy as jnp
from jax import lax

V = 8
C = 32
CONV = 8
DEPTHS = 96
ROWS = 8
W = 1024
SMAX = 127


def draw_raw_views(key, part):
    key_one, key_two = jax.random.split(jax.random.fold_in(key, 3), 2)
    column_ids = jnp.arange(W, dtype=jnp.int32)
    columns = column_ids.astype(jnp.float32) / W
    basic_draw = jnp.clip(jax.random.normal(key_one, (V, C, ROWS, W), jnp.float32), -4.0, 4.0)
    col_scale = jnp.exp(math.log(3.0) * columns + jax.random.uniform(key_two, (W,), jnp.float32, 0.0, math.log(4.0)))
    values = basic_draw * col_scale
    return values.astype(jnp.bfloat16)


def draw_shifts(key, part):
    key_one, key_two, key_three = jax.random.split(jax.random.fold_in(key, 11), 3)
    baseline = jax.random.randint(key_one, (V,), SMAX // 2, SMAX + 1)
    forced = jax.random.randint(key_two, (), 1, V)
    views = jnp.arange(V, dtype=jnp.int32)
    baseline = jnp.where(views == forced, SMAX, baseline)
    jitter = jax.random.randint(key_three, (V, DEPTHS), 0, DEPTHS - 1)
    depth_index = jnp.arange(DEPTHS, dtype=jnp.int32)
    result = (depth_index[None, :] * baseline[:, None] + jitter) // (DEPTHS - 1)
    return jnp.where(views[:, None] == 0, 0, result).astype(jnp.int32)


def draw_frame_range(key, part):
    key_one, key_two = jax.random.split(jax.random.fold_in(key, 17), 2)
    lower = jax.random.randint(key_one, (V,), 0, W // 4 + 1)
    upper = jax.random.randint(key_two, (V,), W - W // 4, W + 1)
    views = jnp.arange(V, dtype=jnp.int32)
    lower = jnp.where(views == 0, 0, lower)
    upper = jnp.where(views == 0, W, upper)
    return jnp.stack([lower, upper], axis=1).astype(jnp.int32)


def draw_final_weight(key, part):
    key_one = jax.random.fold_in(key, 23)
    factor = 4.0
    basic_draw = jnp.clip(jax.random.normal(key_one, (27, CONV), jnp.float32), -4.0, 4.0)
    return (basic_draw * factor / math.sqrt(27.0 * CONV)).astype(jnp.bfloat16)


def bell_draw(own_key, shape, scale, limit, kind=jnp.bfloat16):
    values = jax.random.normal(own_key, shape, jnp.float32) * scale
    return jnp.minimum(jnp.maximum(values, -limit), limit).astype(kind)


def setup_inputs(seed: int = 0) -> dict:
    streams_of = jax.random.split(jax.random.key(seed), 8)
    return {
        "raw_views": draw_raw_views(jax.random.fold_in(streams_of[7], 71), 0),
        "feat_weight": bell_draw(streams_of[1], (9, C, C), (9 * C) ** -0.5, 0.375),
        "shifts": draw_shifts(jax.random.fold_in(streams_of[7], 71), 0),
        "frame_range": draw_frame_range(jax.random.fold_in(streams_of[7], 71), 0),
        "cost_weight": bell_draw(streams_of[4], (27, CONV, C), (27 * C) ** -0.5, 0.21875),
        "mid_weight": bell_draw(streams_of[5], (27, CONV, CONV), (27 * CONV) ** -0.5, 0.4375),
        "final_weight": draw_final_weight(jax.random.fold_in(streams_of[7], 71), 0),
    }


norm_eps = 1e-05

def feature_conv(raw_views, feat_weight):
    row_count = raw_views.shape[2]
    col_total = raw_views.shape[3]
    padded = jnp.pad(raw_views.astype(jnp.float32), ((0, 0), (0, 0), (1, 1), (1, 1)))
    summed = jnp.zeros((raw_views.shape[0], feat_weight.shape[1], row_count, col_total), jnp.float32)
    for kernel_tap in range(9):
        row_off = kernel_tap // 3
        col_off = kernel_tap % 3
        window = padded[:, :, row_off:row_off + row_count, col_off:col_off + col_total]
        summed = summed + jnp.einsum('oi,vihw->vohw', feat_weight[kernel_tap].astype(jnp.float32), window)
    return summed.astype(jnp.bfloat16)

def cost_slice(features, shifts, frame_range, depth_idx):
    depths_all = shifts.shape[1]
    col_total = features.shape[3]
    clipped = jnp.clip(depth_idx, 0, depths_all - 1).astype(jnp.int32)
    view_shift = shifts[:, clipped]
    columns = jnp.arange(col_total, dtype=jnp.int32)
    source = columns[None, :] - view_shift[:, None]
    index_map = jnp.clip(source, 0, col_total - 1).astype(jnp.int32)
    moved = jax.vmap(lambda plane, where_cols: jnp.take(plane, where_cols, axis=2))(features, index_map)
    inside = (source >= frame_range[:, 0:1]) & (source < frame_range[:, 1:2])
    weight_mask = inside.astype(jnp.float32)[:, None, None, :]
    tally = lax.optimization_barrier(jnp.sum(weight_mask, axis=0))
    values = moved.astype(jnp.float32)
    average = lax.optimization_barrier(jnp.sum(weight_mask * values, axis=0)) / tally
    deviation = values - average
    spread = lax.optimization_barrier(jnp.sum(weight_mask * deviation * deviation, axis=0)) / tally
    keep = (depth_idx >= 0) & (depth_idx < depths_all)
    return jnp.where(keep, spread, 0.0).astype(jnp.bfloat16)

def conv_taps(window, weights, amount, row_count, col_count):
    summed = None
    for kernel_tap in range(27):
        depth_off = kernel_tap // 9
        row_off = kernel_tap // 3 % 3
        col_off = kernel_tap % 3
        portion = window[depth_off:depth_off + amount, :, row_off:row_off + row_count, col_off:col_off + col_count]
        term = jnp.einsum('oi,dihw->dohw', weights[kernel_tap].astype(jnp.float32), portion.astype(jnp.float32))
        summed = term if summed is None else summed + term
    return summed

def normalize(values):
    average = lax.optimization_barrier(jnp.mean(values, axis=(0, 2, 3)))
    centered = values - average[None, :, None, None]
    spread = lax.optimization_barrier(jnp.mean(centered * centered, axis=(0, 2, 3)))
    return jnp.maximum(centered * lax.rsqrt(spread + norm_eps)[None, :, None, None], 0.0).astype(jnp.bfloat16)

def conv_full(values, weights):
    depths_all, channels, row_count, col_total = values.shape
    block_len = 8
    padded = jnp.pad(values, ((1, 1), (0, 0), (1, 1), (1, 1)))

    def one_block(index):
        window = lax.dynamic_slice_in_dim(padded, (index * block_len).astype(jnp.int32), block_len + 2, 0)
        return conv_taps(window, weights, block_len, row_count, col_total)
    stacked = lax.map(one_block, jnp.arange(depths_all // block_len, dtype=jnp.int32))
    return stacked.reshape(depths_all, weights.shape[1], row_count, col_total)

def reference(raw_views, feat_weight, shifts, frame_range, cost_weight, mid_weight, final_weight):
    depths_all = shifts.shape[1]
    row_count = raw_views.shape[2]
    col_total = raw_views.shape[3]
    features = feature_conv(raw_views, feat_weight)
    block_len = 8

    def cost_block(index):
        start = (index * block_len).astype(jnp.int32)
        volume = lax.map(lambda depth_step: cost_slice(features, shifts, frame_range, start - 1 + depth_step), jnp.arange(block_len + 2, dtype=jnp.int32))
        framed = jnp.pad(volume, ((0, 0), (0, 0), (1, 1), (1, 1)))
        return conv_taps(framed, cost_weight, block_len, row_count, col_total)
    first_conv = lax.map(cost_block, jnp.arange(depths_all // block_len, dtype=jnp.int32))
    first_conv = first_conv.reshape(depths_all, cost_weight.shape[1], row_count, col_total)
    first_act = normalize(first_conv)
    second_act = normalize(conv_full(first_act, mid_weight))
    score = conv_full(second_act, final_weight[:, None, :])[:, 0]
    peak_value = lax.optimization_barrier(jnp.max(score, axis=0))
    exponent = jnp.exp(score - peak_value[None])
    depth_value = jnp.arange(depths_all, dtype=jnp.float32) / (depths_all - 1)
    return lax.optimization_barrier(jnp.sum(exponent * depth_value[:, None, None], axis=0)) / lax.optimization_barrier(jnp.sum(exponent, axis=0))
```

```python
import functools
import jax
import jax.numpy as jnp
from jax import lax
from jax.experimental import pallas as pl
from jax.experimental.pallas import tpu as pltpu
from jax.sharding import PartitionSpec as P

norm_eps = 1e-05
LANES = 128
ROWS = 8
f32 = jnp.float32
bf16 = jnp.bfloat16
MESH = pl.DeviceIdType.MESH
vmem = pl.BlockSpec(memory_space=pltpu.VMEM)
smem = pl.BlockSpec(memory_space=pltpu.SMEM)


def dot(a, b):
    return jnp.dot(a, b, preferred_element_type=f32)


def iota(shape, dim):
    return lax.broadcasted_iota(jnp.int32, shape, dim)


def remote(src, dst, send, recv, depth, col):
    return pltpu.make_async_remote_copy(
        src_ref=src,
        dst_ref=dst,
        send_sem=send,
        recv_sem=recv,
        device_id=(depth, col),
        device_id_type=MESH,
    )


def tree_sum(parts):
    while len(parts) > 1:
        paired = [a + b for a, b in zip(parts[::2], parts[1::2])]
        parts = paired + parts[len(paired) * 2 :]
    return parts[0]


def spread_rows(table):
    pieces = [
        jnp.broadcast_to(table[o : o + 1], (ROWS, table.shape[1])) for o in range(table.shape[0])
    ]
    return jnp.concatenate(pieces, axis=0)


def expand(weight_ref, table_ref, taps_last):
    wide = table_ref.shape[-1]
    spread = iota((wide // ROWS, wide), 1) // ROWS == iota((wide // ROWS, wide), 0)
    spread = jnp.where(spread, 1.0, 0.0).astype(bf16)
    if taps_last:
        for o in range(weight_ref.shape[0]):
            table_ref[o] = lax.dot_general(
                weight_ref[o], spread, (((0,), (0,)), ((), ())), preferred_element_type=f32
            )
        return
    for tap in range(weight_ref.shape[0]):
        table_ref[tap] = dot(weight_ref[tap], spread)


def row_bands(width):
    out_row = iota((ROWS, width), 0)
    in_row = lax.rem(iota((ROWS, width), 1), ROWS)
    return [in_row - out_row + 1 == b for b in range(3)]


def banded(table_ref, count, first, step, bands, taps_last):
    pieces = []
    for o in range(count):
        block = jnp.zeros(bands[0].shape, f32)
        for b in range(3):
            tap = first + step * b
            row = table_ref[o, tap : tap + 1, :] if taps_last else table_ref[tap, o : o + 1, :]
            block = jnp.where(bands[b], jnp.broadcast_to(row, block.shape), block)
        pieces.append(block)
    return jnp.concatenate(pieces, axis=0) if count > 1 else pieces[0]


def build_conv(table_ref, count, wide, mat_ref, taps_last):
    bands = row_bands(wide)
    high = count * ROWS
    for a in range(3):
        for e in range(3):
            block = banded(table_ref, count, 9 * a + e, 3, bands, taps_last)
            mat_ref[e * high : (e + 1) * high, a * wide : (a + 1) * wide] = block.astype(
                mat_ref.dtype
            )


def feature_stage(
    depths, cols, ready, raw_views, feat_weight, cost_weight, mid_weight, final_weight, own, left, right,
    edge, cost_mat, mid_mat, final_mat, raw, table, cost_table, mid_table, final_table, raw_left, raw_right,
    mat, s_raw, r_raw, s_dep, r_dep,
    s_right, r_right, s_left, r_left
):
    me, col = lax.axis_index("depth"), lax.axis_index("col")
    count, high, n = raw.shape
    channels = high // ROWS
    has_left, has_right = col > 0, col < cols - 1
    raw[...] = raw_views[...].reshape(raw.shape)
    expand(feat_weight, table, False)
    bands = row_bands(high)
    for e in range(3):
        mat[e * high : (e + 1) * high, :] = banded(
            table, channels, e, 3, bands, False
        ).astype(bf16)
    ready()

    def edge_right():
        return remote(
            raw.at[:, :, n - LANES : n], raw_left, s_raw.at[0], r_raw.at[0], me, col + 1
        )

    def edge_left():
        return remote(raw.at[:, :, 0:LANES], raw_right, s_raw.at[1], r_raw.at[1], me, col - 1)

    pl.when(has_right)(lambda: edge_right().start())
    pl.when(has_left)(lambda: edge_left().start())
    for weight, spread, built, taps_last in (
        (cost_weight, cost_table, cost_mat, False),
        (mid_weight, mid_table, mid_mat, True),
        (final_weight, final_table, final_mat, True),
    ):
        expand(weight, spread, taps_last)
        build_conv(spread, built.shape[0] // (3 * ROWS), built.shape[1] // 3, built, taps_last)
    pl.when(has_left)(lambda: edge_right().wait_recv())
    pl.when(has_right)(lambda: edge_left().wait_recv())

    for v in range(count):
        before = jnp.where(has_left, raw_left[v].astype(f32), 0.0).astype(bf16)
        after = jnp.where(has_right, raw_right[v].astype(f32), 0.0).astype(bf16)
        wide = jnp.concatenate([before, raw[v], after], axis=1)
        total = None
        for e in range(3):
            part = dot(mat[e * high : (e + 1) * high, :], wide)
            part = pltpu.roll(part, (1 - e) % part.shape[1], 1)[:, LANES : LANES + n]
            total = part if total is None else total + part
        own[me * count + v] = total.astype(bf16)

    def to_depth(k, slot):
        part = pl.ds(slot * count, count)
        return remote(
            own.at[part], own.at[part], s_dep.at[k], r_dep.at[slot], lax.rem(me + k, depths), col
        )

    def to_right(k, slot):
        part = pl.ds(slot * count, count)
        return remote(
            own.at[part, :, n - LANES : n], left.at[part], s_right.at[k], r_right.at[slot], me, col + 1
        )

    def to_left():
        return remote(edge, right, s_left.at[0], r_left.at[0], me, col - 1)

    for k in range(1, depths):
        to_depth(k, me).start()
    for k in range(depths):
        slot = lax.rem(me + k, depths)
        if k:
            to_depth(k, slot).wait_recv()
        pl.when(has_right)(lambda: to_right(k, slot).start())
    lane = iota((high, LANES), 1)
    packed = jnp.zeros((high, LANES), bf16)
    for v in range(depths * count):
        first = own[v, :, 0:LANES]
        packed = jnp.where(lane == v, pltpu.roll(first, v, 1) if v else first, packed)
    edge[...] = packed
    pl.when(has_left)(lambda: to_left().start())
    for k in range(1, depths):
        to_depth(k, me).wait_send()
    pl.when(has_right)(lambda: edge_right().wait_send())
    pl.when(has_left)(lambda: edge_left().wait_send())
    for k in range(depths):
        slot = lax.rem(me + k, depths)
        pl.when(has_right)(lambda: to_right(k, slot).wait_send())
        pl.when(has_left)(lambda: to_right(k, slot).wait_recv())
    pl.when(has_left)(lambda: to_left().wait_send())
    pl.when(has_right)(lambda: to_left().wait_recv())


def convolve(slab, wide, mat, halo_left, halo_right, high, depth_local, out, pack_left, pack_right,
             stats):
    n = slab.shape[1]
    tiles = n // LANES
    edge_left = edge_right = None
    for a in range(3):
        w_a = mat[0:high, a * wide : (a + 1) * wide]
        w_b = mat[2 * high : 3 * high, a * wide : (a + 1) * wide]
        part_a = pltpu.roll(dot(w_a, halo_left), (LANES - a) % LANES, 1)
        part_b = pltpu.roll(dot(w_b, halo_right), (LANES - a) % LANES, 1)
        edge_left = part_a if edge_left is None else edge_left + part_a
        edge_right = part_b if edge_right is None else edge_right + part_b
    lane = iota((high, LANES), 1)
    column = iota((high, n), 1)
    half = depth_local // 2
    weights = mat[...]

    def over_tiles(x):
        return jnp.concatenate([x] * tiles, axis=1) if tiles > 1 else x

    def one_step(t, carry):
        halves = []
        for g in range(2):
            start = pl.multiple_of((t + g * half) * wide, wide)
            halves.append(slab[pl.ds(start, 3 * wide), :])
        product = dot(weights, jnp.concatenate(halves, axis=1))
        carry = list(carry)
        for g in range(2):
            d = t + g * half
            part = product[:, g * n : (g + 1) * n]
            from_left = pltpu.roll(part[0:high], 1, 1)
            from_right = pltpu.roll(part[2 * high : 3 * high], n - 1, 1)
            rim_left = over_tiles(pltpu.roll(edge_left, lax.rem(LANES - d, LANES), 1))
            rim_right = over_tiles(pltpu.roll(edge_right, LANES - 1 - d, 1))
            result = (
                jnp.where(column == 0, rim_left, from_left)
                + part[high : 2 * high]
                + jnp.where(column == n - 1, rim_right, from_right)
            )
            out[d] = result
            if stats is not None:
                carry[0] = carry[0] + result
                carry[1] = carry[1] + result * result
                carry[2] = jnp.where(lane == d, pltpu.roll(result[:, 0:LANES], d, 1), carry[2])
                carry[3] = jnp.where(
                    lane == d, pltpu.roll(result[:, n - LANES : n], d + 1, 1), carry[3]
                )
        return tuple(carry)

    if stats is None:
        lax.fori_loop(0, half, one_step, (), unroll=4)
        return
    wide_zero = jnp.zeros((high, n), f32)
    lane_zero = jnp.zeros((high, LANES), f32)
    first, second, pack_l, pack_r = lax.fori_loop(
        0, half, one_step, (wide_zero, wide_zero, lane_zero, lane_zero), unroll=2
    )
    pack_left[...] = pack_l
    pack_right[...] = pack_r

    def per_channel(x):
        x = sum(x[:, j * LANES : (j + 1) * LANES] for j in range(tiles))
        rows = [
            jnp.sum(x[o * ROWS : (o + 1) * ROWS], axis=0, keepdims=True)
            for o in range(high // ROWS)
        ]
        return jnp.concatenate(rows, axis=0)

    count = high // ROWS
    spot = iota((count, LANES), 1) - iota((count, LANES), 0)
    total = jnp.sum(per_channel(first), axis=1, keepdims=True)
    squares = jnp.sum(per_channel(second), axis=1, keepdims=True)
    row = jnp.where(spot == 0, total, jnp.where(spot == count, squares, 0.0))
    stats[...] = jnp.sum(row, axis=0, keepdims=True)


def volume_stage(
    depth_total, depth_local, cols, own, left, right, edge, shifts, frame, shift_rows, mat, out, pack_left,
    pack_right, stats, feats, slab, halo_views
):
    views, high, n = own.shape
    channels = high // ROWS
    first_depth = lax.axis_index("depth") * depth_local
    first_col = lax.axis_index("col") * n
    for v in range(views):
        for at, piece in ((0, left[v]), (LANES, own[v])):
            c = first_col - LANES + at + iota(piece.shape, 1)
            seen = (c >= frame[0, v]) & (c < frame[1, v])
            feats[v, :, at : at + piece.shape[1]] = jnp.where(seen, piece, jnp.zeros_like(piece))
    lane = iota((ROWS, LANES), 1)
    pair_lane = iota((2 * ROWS, LANES), 1)

    def one_depth(step, _):
        depth = first_depth + step - 1
        valid = (depth >= 0) & (depth < depth_total)
        clipped = jnp.clip(depth, 0, depth_total - 1)
        moves = [shifts[v, clipped] for v in range(views)]
        for j in range(n // LANES):
            x = first_col + j * LANES + lane
            wraps = []
            tally = jnp.zeros((ROWS, LANES), f32)
            for v in range(views):
                c = x - moves[v]
                mask = (c >= frame[0, v]) & (c < frame[1, v])
                tally = tally + jnp.where(mask, 1.0, 0.0)
                wraps.append(pair_lane >= LANES - moves[v])
            scale = 1.0 / tally
            absent = views - tally
            last_scale = jnp.where(valid, scale, 0.0)
            scale, absent, last_scale = [
                jnp.concatenate([part, part], axis=0) for part in (scale, absent, last_scale)
            ]

            def one_pair(pair, _):
                rows = pl.ds(pl.multiple_of(pair * 2 * ROWS, 2 * ROWS), 2 * ROWS)
                vals = []
                for v in range(views):
                    value = feats[v, rows, (j + 1) * LANES : (j + 2) * LANES]
                    if v:
                        behind = feats[v, rows, j * LANES : (j + 1) * LANES]
                        value = pltpu.roll(jnp.where(wraps[v], behind, value), moves[v], 1)
                    vals.append(value.astype(f32))
                average = tree_sum(vals) * scale
                square = tree_sum([(value - average) * (value - average) for value in vals])
                square = jnp.maximum(square - absent * (average * average), 0.0) * last_scale
                where_to = pl.ds(pl.multiple_of(step * high + pair * 2 * ROWS, 2 * ROWS), 2 * ROWS)
                slab[where_to, j * LANES : (j + 1) * LANES] = square.astype(bf16)
                return _

            lax.fori_loop(0, channels // 2, one_pair, 0, unroll=True)
        return _

    lax.fori_loop(0, depth_local + 2, one_depth, 0, unroll=2)

    view_lane = iota(right.shape, 1)
    ahead = jnp.zeros(right.shape, bf16)
    for v in range(views):
        c = first_col + n
        seen = (c >= frame[0, v]) & (c < frame[1, v]) & (view_lane == v)
        ahead = jnp.where(seen, right[...], ahead)
    halos = []
    padding = jnp.zeros((views, LANES - depth_total), jnp.int32)
    lane_shifts = pltpu.roll(
        jnp.concatenate([shift_rows[...], padding], axis=1),
        lax.rem(LANES + 1 - first_depth, LANES),
        1,
    )
    lane_row = iota((1, LANES), 1)
    depth_row = first_depth + lane_row - 1
    for side in range(2):
        x = first_col - 1 if side == 0 else first_col + n
        for v in range(views):
            shift_row = lane_shifts[v : v + 1, :]
            row_id = iota((LANES, LANES), 0)
            if side == 0:
                source, base = feats[v, :, 0:LANES], LANES - 1
            else:
                source, base = feats[v, :, n : n + LANES], LANES
            pick = row_id == base - shift_row
            found = dot(source, jnp.where(pick, 1.0, 0.0).astype(bf16))
            if side:
                pick = (row_id == v) & (shift_row == 0)
                found = found + dot(ahead, jnp.where(pick, 1.0, 0.0).astype(bf16))
            halo_views[v] = found
        tally = jnp.zeros((1, LANES), f32)
        for v in range(views):
            c = x - lane_shifts[v : v + 1, :]
            tally = tally + jnp.where((c >= frame[0, v]) & (c < frame[1, v]), 1.0, 0.0)
        scale = 1.0 / jnp.maximum(tally, 1.0)
        keep = (depth_row >= 0) & (depth_row < depth_total) & (lane_row < depth_local + 2)
        keep = keep & (x >= 0) & (x < n * cols)
        total = jnp.zeros((high, LANES), f32)
        for v in range(views):
            total = total + halo_views[v]
        average = total * scale
        square = jnp.zeros((high, LANES), f32)
        for v in range(views):
            dev = halo_views[v] - average
            square = square + dev * dev
        square = jnp.maximum(square - (views - tally) * (average * average), 0.0)
        halos.append(jnp.where(keep, square * scale, 0.0).astype(bf16))
    convolve(
        slab, high, mat, halos[0], halos[1], 8 * ROWS, depth_local, out, pack_left, pack_right, stats
    )


def exchange(
    depths, cols, voxels, conv, pack_left, pack_right, stats, slab, plane_low, plane_high, from_left,
    from_right, others, s_near, r_near, s_all, r_all, known=None
):
    me, col = lax.axis_index("depth"), lax.axis_index("col")
    depth_local, high, n = conv.shape
    has_left, has_right = col > 0, col < cols - 1
    has_low, has_high = me > 0, me < depths - 1
    def to_all(k):
        kd, kc = k // cols, lax.rem(k, cols)
        return remote(
            stats, others.at[k - 1], s_all.at[0], r_all.at[0], lax.rem(me + kd, depths),
            lax.rem(col + kc, cols)
        )

    if known is not None:
        known()
    if depths * cols > 64:
        lax.fori_loop(1, depths * cols, lambda k, _: (to_all(k).start(), _)[1], 0)
    else:
        for k in range(1, depths * cols):
            to_all(jnp.int32(k)).start()
    near = []
    down = lambda: remote(conv.at[0], plane_high, s_near.at[0], r_near.at[0], me - 1, col)
    up = lambda: remote(
        conv.at[depth_local - 1], plane_low, s_near.at[1], r_near.at[1], me + 1, col
    )
    near.append((down, has_low, has_high))
    near.append((up, has_high, has_low))
    always = col >= 0
    for i, (dd, ok, back) in enumerate(
        ((-1, has_low, has_high), (0, always, always), (1, has_high, has_low))
    ):
        near.append(
            (
                lambda dd=dd, i=i: remote(
                    pack_right, from_left.at[1 - dd], s_near.at[2 + i], r_near.at[2 + i], me + dd, col + 1
                ),
                ok & has_right,
                back & has_left,
            )
        )
        near.append(
            (
                lambda dd=dd, i=i: remote(
                    pack_left, from_right.at[1 - dd], s_near.at[5 + i], r_near.at[5 + i], me + dd, col - 1
                ),
                ok & has_left,
                back & has_right,
            )
        )
    for copy, sends, _ in near:
        pl.when(sends)(lambda copy=copy: copy().start())

    for copy, _, receives in near:
        pl.when(receives)(lambda copy=copy: copy().wait_recv())
    everyone = remote(others, others, s_all.at[0], r_all.at[0], me, col)
    everyone.wait_recv()
    count = high // ROWS
    sums = jnp.broadcast_to(jnp.sum(others[...], axis=0) + stats[...], (count, LANES))
    spot = iota((count, LANES), 1) - iota((count, LANES), 0)

    def pick(at):
        return jnp.sum(jnp.where(spot == at, sums, 0.0), axis=1, keepdims=True) / voxels

    average = pick(0)
    variance = pick(count) - average * average
    average = spread_rows(jnp.broadcast_to(average, (high // ROWS, LANES)))
    factor = spread_rows(jnp.broadcast_to(lax.rsqrt(variance + norm_eps), (high // ROWS, LANES)))

    def activate(x):
        return jnp.maximum((x - average) * factor, 0.0)

    def activate_plane(x):
        parts = [activate(x[:, j * LANES : (j + 1) * LANES]) for j in range(n // LANES)]
        return jnp.concatenate(parts, axis=1) if len(parts) > 1 else parts[0]

    slab[0:high, :] = jnp.where(has_low, activate_plane(plane_low[...]), 0.0).astype(bf16)
    slab[(depth_local + 1) * high : (depth_local + 2) * high, :] = jnp.where(
        has_high, activate_plane(plane_high[...]), 0.0
    ).astype(bf16)

    def one_plane(d, _):
        slab[pl.ds(pl.multiple_of((d + 1) * high, high), high), :] = activate_plane(conv[d]).astype(
            bf16
        )
        return _

    lax.fori_loop(0, depth_local, one_plane, 0, unroll=2)
    lane = iota((high, LANES), 1)
    halos = []
    for parts, ok in ((from_left, has_left), (from_right, has_right)):
        low = pltpu.roll(parts[0], LANES - (depth_local - 1), 1)
        mid = pltpu.roll(parts[1], 1, 1)
        top = pltpu.roll(parts[2], depth_local + 1, 1)
        row = jnp.where(lane == 0, low, jnp.where(lane == depth_local + 1, top, mid))
        keep = ok & (lane <= depth_local + 1)
        keep = keep & (has_low | (lane > 0)) & (has_high | (lane < depth_local + 1))
        halos.append(jnp.where(keep, activate(row), 0.0).astype(bf16))

    def finish():
        everyone.wait_send()
        for copy, sends, _ in near:
            pl.when(sends)(lambda copy=copy: copy().wait_send())

    return halos, finish


def score_stage(
    depths, cols, voxels, depth_total, conv, pack_left, pack_right, stats, mat, out, score, parts,
    s_part, r_part, slab, *rest
):
    me, col = lax.axis_index("depth"), lax.axis_index("col")
    depth_local, high, n = conv.shape
    halos, finish = exchange(
        depths, cols, voxels, conv, pack_left, pack_right, stats, slab, *rest
    )
    convolve(slab, high, mat, halos[0], halos[1], ROWS, depth_local, score, None, None, None)
    planes = [score[d] for d in range(depth_local)]
    peak = functools.reduce(jnp.maximum, planes)
    total = jnp.zeros_like(peak)
    weighted = jnp.zeros_like(peak)
    first_depth = me * depth_local
    for d in range(depth_local):
        term = jnp.exp(planes[d] - peak)
        total = total + term
        weighted = weighted + term * ((first_depth + d).astype(f32) / (depth_total - 1))
    parts[me, 0] = peak
    parts[me, 1] = total
    parts[me, 2] = weighted

    def to_depth(k, slot):
        return remote(
            parts.at[slot], parts.at[slot], s_part.at[k], r_part.at[slot], lax.rem(me + k, depths), col
        )

    for k in range(1, depths):
        to_depth(k, me).start()
    for k in range(1, depths):
        to_depth(k, lax.rem(me + k, depths)).wait_recv()
    highest = functools.reduce(jnp.maximum, [parts[p, 0] for p in range(depths)])
    total = jnp.zeros_like(highest)
    weighted = jnp.zeros_like(highest)
    for p in range(depths):
        scale = jnp.exp(parts[p, 0] - highest)
        total = total + parts[p, 1] * scale
        weighted = weighted + parts[p, 2] * scale
    out[...] = weighted / total
    finish()
    for k in range(1, depths):
        to_depth(k, me).wait_send()


def whole_kernel(groups, depths, cols, voxels, depth_total, depth_local, *refs):
    (
        raw_views, feat_weight, cost_weight, mid_weight, final_weight, shifts, frame, shift_rows, out
    ) = refs[:9]
    rest, taken = [], 9
    for size in groups:
        rest.append(refs[taken : taken + size])
        taken += size
    gathered, mats, feature_refs, volume_refs, first, second, swap_a, swap_b, score_refs, known = rest
    known_sem = known[0]
    me, col = lax.axis_index("depth"), lax.axis_index("col")
    has_left, has_right = col > 0, col < cols - 1
    has_low, has_high = me > 0, me < depths - 1
    count = lambda flag: flag.astype(jnp.int32)
    barrier = pltpu.get_barrier_semaphore()

    def greet(d, c):
        pl.semaphore_signal(barrier, inc=1, device_id=(d, c), device_id_type=MESH)

    for k in range(1, depths):
        greet(lax.rem(me + k, depths), col)
    for k in range(1, cols):
        greet(me, lax.rem(col + k, cols))
    for dd, ok_d in ((-1, has_low), (1, has_high)):
        for dc, ok_c in ((-1, has_left), (1, has_right)):
            pl.when(ok_d & ok_c)(lambda dd=dd, dc=dc: greet(me + dd, col + dc))
    diagonals = (count(has_low) + count(has_high)) * (count(has_left) + count(has_right))

    def ready():
        pl.semaphore_wait(barrier, depths - 1 + cols - 1 + diagonals)
        for k in range(1, cols):
            pl.semaphore_signal(
                known_sem, inc=1, device_id=(me, lax.rem(col + k, cols)), device_id_type=MESH
            )

    def all_known():
        pl.semaphore_wait(known_sem, cols - 1)

    feature_stage(
        depths, cols, ready, raw_views, feat_weight, cost_weight, mid_weight, final_weight, *gathered,
        *mats, *feature_refs
    )
    volume_stage(
        depth_total, depth_local, cols, *gathered, shifts, frame, shift_rows, mats[0], *first,
        *volume_refs
    )
    halos, finish = exchange(depths, cols, voxels, *first, *swap_a, all_known)
    high = first[0].shape[1]
    convolve(swap_a[0], high, mats[1], halos[0], halos[1], high, depth_local, *second)
    finish()
    score_stage(depths, cols, voxels, depth_total, *second, mats[2], out, *score_refs, *swap_b)


def buffer(dims, kind):
    return pltpu.VMEM(dims, kind)


def dma(n):
    return pltpu.SemaphoreType.DMA((n,))


def local(raw_views, feat_weight, shifts, frame_range, cost_weight, mid_weight, final_weight):
    view_local, channels, rows, n = raw_views.shape
    depths, cols = lax.axis_size("depth"), lax.axis_size("col")
    views, depth_total = shifts.shape
    depth_local = depth_total // depths
    high = channels * rows
    hidden = cost_weight.shape[1]
    mid_high = hidden * rows
    voxels = float(depth_total * rows * n * cols)

    gathered = [
        buffer((views, high, n), bf16),
        buffer((views, high, LANES), bf16),
        buffer((high, LANES), bf16),
        buffer((high, LANES), bf16),
    ]
    mats = [
        buffer((3 * mid_high, 3 * high), bf16),
        buffer((3 * mid_high, 3 * mid_high), bf16),
        buffer((3 * rows, 3 * mid_high), bf16),
    ]
    feature_refs = [
        buffer((view_local, high, n), bf16),
        buffer((9, channels, high), f32),
        buffer((27, hidden, high), f32),
        buffer((hidden, 27, mid_high), f32),
        buffer((1, 27, mid_high), f32),
        buffer((view_local, high, LANES), bf16),
        buffer((view_local, high, LANES), bf16),
        buffer((3 * high, high), bf16),
        dma(2), dma(2), dma(depths), dma(depths), dma(depths), dma(depths), dma(1), dma(1),
    ]
    volume_refs = [
        buffer((views, high, n + LANES), bf16),
        buffer(((depth_local + 2) * high, n), bf16),
        buffer((views, high, LANES), f32),
    ]

    def conv_refs():
        return [
            buffer((depth_local, mid_high, n), f32),
            buffer((mid_high, LANES), f32),
            buffer((mid_high, LANES), f32),
            buffer((1, LANES), f32),
        ]

    def swap_refs():
        return [
            buffer(((depth_local + 2) * mid_high, n), bf16),
            buffer((mid_high, n), f32),
            buffer((mid_high, n), f32),
            buffer((3, mid_high, LANES), f32),
            buffer((3, mid_high, LANES), f32),
            buffer((depths * cols - 1, 1, LANES), f32),
            dma(8), dma(8), dma(1), dma(1),
        ]

    score_refs = [
        buffer((depth_local, rows, n), f32),
        buffer((depths, 3, rows, n), f32),
        dma(depths), dma(depths),
    ]
    groups = [
        gathered, mats, feature_refs, volume_refs, conv_refs(), conv_refs(), swap_refs(), swap_refs(),
        score_refs, [pltpu.SemaphoreType.REGULAR],
    ]
    return pl.pallas_call(
        functools.partial(
            whole_kernel, [len(g) for g in groups], depths, cols, voxels, depth_total, depth_local
        ),
        out_shape=jax.ShapeDtypeStruct((rows, n), f32),
        in_specs=[vmem] * 5 + [smem] * 2 + [vmem],
        out_specs=vmem,
        scratch_shapes=[ref for g in groups for ref in g],
        compiler_params=pltpu.CompilerParams(collective_id=0, has_side_effects=True),
        name="whole",
    )(
        raw_views, feat_weight, cost_weight, jnp.transpose(mid_weight, (1, 2, 0)),
        jnp.transpose(final_weight)[None], shifts, jnp.transpose(frame_range), shifts
    )


def solution(mesh):
    in_specs = (P("depth", None, None, "col"), P(), P(), P(), P(), P(), P())
    out_specs = P(None, "col")
    return jax.shard_map(local, mesh=mesh, in_specs=in_specs, out_specs=out_specs, check_vma=False)
```

```python
import functools
import jax
import jax.numpy as jnp
from jax import lax
from jax.experimental import pallas as pl
from jax.experimental.pallas import tpu as pltpu
from jax.sharding import PartitionSpec as P

norm_eps = 1e-05
LANES = 128
ROWS = 8
f32 = jnp.float32
bf16 = jnp.bfloat16
MESH = pl.DeviceIdType.MESH
vmem = pl.BlockSpec(memory_space=pltpu.VMEM)
smem = pl.BlockSpec(memory_space=pltpu.SMEM)


def dot(a, b):
    return jnp.dot(a, b, preferred_element_type=f32)


def iota(shape, dim):
    return lax.broadcasted_iota(jnp.int32, shape, dim)


def remote(src, dst, send, recv, depth, col):
    return pltpu.make_async_remote_copy(
        src_ref=src,
        dst_ref=dst,
        send_sem=send,
        recv_sem=recv,
        device_id=(depth, col),
        device_id_type=MESH,
    )


def tree_sum(parts):
    while len(parts) > 1:
        paired = [a + b for a, b in zip(parts[::2], parts[1::2])]
        parts = paired + parts[len(paired) * 2 :]
    return parts[0]


def spread_rows(table):
    pieces = [
        jnp.broadcast_to(table[o : o + 1], (ROWS, table.shape[1])) for o in range(table.shape[0])
    ]
    return jnp.concatenate(pieces, axis=0)


def expand(weight_ref, table_ref, taps_last):
    wide = table_ref.shape[-1]
    spread = iota((wide // ROWS, wide), 1) // ROWS == iota((wide // ROWS, wide), 0)
    spread = jnp.where(spread, 1.0, 0.0).astype(bf16)
    if taps_last:
        for o in range(weight_ref.shape[0]):
            table_ref[o] = lax.dot_general(
                weight_ref[o], spread, (((0,), (0,)), ((), ())), preferred_element_type=f32
            )
        return
    for tap in range(weight_ref.shape[0]):
        table_ref[tap] = dot(weight_ref[tap], spread)


def row_bands(width):
    out_row = iota((ROWS, width), 0)
    in_row = lax.rem(iota((ROWS, width), 1), ROWS)
    return [in_row - out_row + 1 == b for b in range(3)]


def banded(table_ref, count, first, step, bands, taps_last):
    pieces = []
    for o in range(count):
        block = jnp.zeros(bands[0].shape, f32)
        for b in range(3):
            tap = first + step * b
            row = table_ref[o, tap : tap + 1, :] if taps_last else table_ref[tap, o : o + 1, :]
            block = jnp.where(bands[b], jnp.broadcast_to(row, block.shape), block)
        pieces.append(block)
    return jnp.concatenate(pieces, axis=0) if count > 1 else pieces[0]


def build_conv(table_ref, count, wide, mat_ref, taps_last):
    bands = row_bands(wide)
    high = count * ROWS
    for a in range(3):
        for e in range(3):
            block = banded(table_ref, count, 9 * a + e, 3, bands, taps_last)
            mat_ref[e * high : (e + 1) * high, a * wide : (a + 1) * wide] = block.astype(
                mat_ref.dtype
            )


def partner(me, depths, k):
    if depths == 4:
        return [me, me + 1 - 2 * lax.rem(me, 2), lax.rem(me + 2, 4), 3 - me][k]
    return lax.rem(me + k, depths)


def origin(me, depths, k):
    return partner(me, depths, k if depths == 4 else (depths - k) % depths)


def feature_stage(
    depths, cols, ready, raw_views, feat_weight, cost_weight, mid_weight, final_weight, frame, own, left,
    right, edge, feats, cost_mat, mid_mat, final_mat, raw, table, cost_table, mid_table, final_table,
    rim, rim_left, rim_right, partial, mat, s_raw, r_raw, s_dep, r_dep, s_right, r_right, s_left, r_left
):
    me, col = lax.axis_index("depth"), lax.axis_index("col")
    count, high, n = raw.shape
    views = depths * count
    channels = high // ROWS
    has_left, has_right = col > 0, col < cols - 1
    first_col = col * n
    lane = iota((high, LANES), 1)
    half = LANES // 2
    raw[...] = raw_views[...].reshape(raw.shape)
    packed = jnp.zeros((high, LANES), bf16)
    for v in range(count):
        first, last = raw[v, :, 0:LANES], raw[v, :, n - LANES : n]
        packed = jnp.where(lane == v, pltpu.roll(first, v, 1) if v else first, packed)
        packed = jnp.where(lane == half + v, pltpu.roll(last, half + v + 1, 1), packed)
    rim[...] = packed
    ready()

    def edge_right():
        return remote(rim, rim_left, s_raw.at[0], r_raw.at[0], me, col + 1)

    def edge_left():
        return remote(rim, rim_right, s_raw.at[1], r_raw.at[1], me, col - 1)

    pl.when(has_right)(lambda: edge_right().start())
    pl.when(has_left)(lambda: edge_left().start())
    expand(feat_weight, table, False)
    bands = row_bands(high)
    for e in range(3):
        mat[e * high : (e + 1) * high, :] = banded(
            table, channels, e, 3, bands, False
        ).astype(bf16)
    column = iota((high, n), 1)
    for v in range(count):
        before = pltpu.roll(dot(mat[0:high, :], raw[v]), 1, 1)
        after = pltpu.roll(dot(mat[2 * high : 3 * high, :], raw[v]), n - 1, 1)
        total = jnp.where(column == 0, 0.0, before) + dot(mat[high : 2 * high, :], raw[v])
        partial[v] = total + jnp.where(column == n - 1, 0.0, after)
    pl.when(has_left)(lambda: edge_right().wait_recv())
    pl.when(has_right)(lambda: edge_left().wait_recv())
    pick = has_left & (lane >= half) & (lane < half + count)
    before = dot(mat[0:high, :], jnp.where(pick, rim_left[...].astype(f32), 0.0).astype(bf16))
    pick = has_right & (lane < count)
    after = dot(
        mat[2 * high : 3 * high, :], jnp.where(pick, rim_right[...].astype(f32), 0.0).astype(bf16)
    )
    zero = jnp.zeros((high, n - LANES), f32)
    for v in range(count):
        low = jnp.where(lane == 0, pltpu.roll(before, half - v, 1), 0.0)
        top = jnp.where(lane == LANES - 1, pltpu.roll(after, LANES - 1 - v, 1), 0.0)
        if n > LANES:
            low = jnp.concatenate([low, zero], axis=1)
            top = jnp.concatenate([zero, top], axis=1)
        own[me * count + v] = (partial[v] + low + top).astype(bf16)

    def to_depth(k, j, slot):
        v = slot * count + j
        return remote(
            own.at[v], own.at[v], s_dep.at[k * count + j], r_dep.at[v], partner(me, depths, k), col
        )

    def to_right(v):
        return remote(
            own.at[v, :, n - LANES : n], left.at[v], s_right.at[v], r_right.at[v], me, col + 1
        )

    def to_left():
        return remote(edge, right, s_left.at[0], r_left.at[0], me, col - 1)

    for k in range(1, depths):
        for j in range(count):
            to_depth(k, j, me).start()
    for j in range(count):
        pl.when(has_right)(lambda j=j: to_right(me * count + j).start())
    for weight, spread, built, taps_last in (
        (cost_weight, cost_table, cost_mat, False),
        (mid_weight, mid_table, mid_mat, True),
        (final_weight, final_table, final_mat, True),
    ):
        expand(weight, spread, taps_last)
        build_conv(spread, built.shape[0] // (3 * ROWS), built.shape[1] // 3, built, taps_last)

    def absorb(v, source, at, width):
        c = first_col - LANES + at + iota((high, width), 1)
        seen = (c >= frame[0, v]) & (c < frame[1, v])
        feats[v, :, at : at + width] = jnp.where(seen, source[v], jnp.zeros((high, width), bf16))

    order = [(k, j) for k in range(depths) for j in range(count)]
    for k, j in order:
        v = origin(me, depths, k) * count + j
        if k:
            to_depth(k, j, origin(me, depths, k)).wait_recv()
            pl.when(has_right)(lambda v=v: to_right(v).start())
        absorb(v, own, LANES, n)
    packed = jnp.zeros((high, LANES), bf16)
    for v in range(views):
        first = own[v, :, 0:LANES]
        packed = jnp.where(lane == v, pltpu.roll(first, v, 1) if v else first, packed)
    edge[...] = packed
    pl.when(has_left)(lambda: to_left().start())
    for k, j in order:
        v = origin(me, depths, k) * count + j
        pl.when(has_left)(lambda v=v: to_right(v).wait_recv())
        absorb(v, left, 0, LANES)
    pl.when(has_right)(lambda: to_left().wait_recv())

    def finish():
        pl.when(has_right)(lambda: edge_right().wait_send())
        pl.when(has_left)(lambda: edge_left().wait_send())
        for k, j in order:
            if k:
                to_depth(k, j, me).wait_send()
            pl.when(has_right)(lambda k=k, j=j: to_right(k * count + j).wait_send())
        pl.when(has_left)(lambda: to_left().wait_send())

    return finish


def convolve(slab, wide, mat, halo_left, halo_right, far, high, depth_local, out, pack_left, pack_right,
             stats):
    n = slab.shape[1]
    tiles = n // LANES
    edge_left = edge_right = None
    for a in range(3):
        w_a = mat[0:high, a * wide : (a + 1) * wide]
        w_b = mat[2 * high : 3 * high, a * wide : (a + 1) * wide]
        part_a = pltpu.roll(dot(w_a, halo_left), (LANES - a) % LANES, 1)
        part_b = pltpu.roll(dot(w_b, halo_right), (LANES - a - far) % LANES, 1)
        edge_left = part_a if edge_left is None else edge_left + part_a
        edge_right = part_b if edge_right is None else edge_right + part_b
    lane = iota((high, LANES), 1)
    column = iota((high, n), 1)
    half = depth_local // 2
    weights = mat[...]

    def over_tiles(x):
        return jnp.concatenate([x] * tiles, axis=1) if tiles > 1 else x

    def one_step(t, carry):
        halves = []
        for g in range(2):
            start = pl.multiple_of((t + g * half) * wide, wide)
            halves.append(slab[pl.ds(start, 3 * wide), :])
        product = dot(weights, jnp.concatenate(halves, axis=1))
        carry = list(carry)
        for g in range(2):
            d = t + g * half
            part = product[:, g * n : (g + 1) * n]
            from_left = pltpu.roll(part[0:high], 1, 1)
            from_right = pltpu.roll(part[2 * high : 3 * high], n - 1, 1)
            rim_left = over_tiles(pltpu.roll(edge_left, lax.rem(LANES - d, LANES), 1))
            rim_right = over_tiles(pltpu.roll(edge_right, LANES - 1 - d, 1))
            result = (
                jnp.where(column == 0, rim_left, from_left)
                + part[high : 2 * high]
                + jnp.where(column == n - 1, rim_right, from_right)
            )
            out[d] = result
            if stats is not None:
                carry[0] = carry[0] + result
                carry[1] = carry[1] + result * result
                carry[2] = jnp.where(lane == d, pltpu.roll(result[:, 0:LANES], d, 1), carry[2])
                carry[3] = jnp.where(
                    lane == d, pltpu.roll(result[:, n - LANES : n], d + 1, 1), carry[3]
                )
        return tuple(carry)

    if stats is None:
        lax.fori_loop(0, half, one_step, (), unroll=4)
        return
    wide_zero = jnp.zeros((high, n), f32)
    lane_zero = jnp.zeros((high, LANES), f32)
    first, second, pack_l, pack_r = lax.fori_loop(
        0, half, one_step, (wide_zero, wide_zero, lane_zero, lane_zero), unroll=2
    )
    pack_left[...] = pack_l
    pack_right[...] = pack_r

    def per_channel(x):
        x = sum(x[:, j * LANES : (j + 1) * LANES] for j in range(tiles))
        rows = [
            jnp.sum(x[o * ROWS : (o + 1) * ROWS], axis=0, keepdims=True)
            for o in range(high // ROWS)
        ]
        return jnp.concatenate(rows, axis=0)

    count = high // ROWS
    spot = iota((count, LANES), 1) - iota((count, LANES), 0)
    total = jnp.sum(per_channel(first), axis=1, keepdims=True)
    squares = jnp.sum(per_channel(second), axis=1, keepdims=True)
    row = jnp.where(spot == 0, total, jnp.where(spot == count, squares, 0.0))
    stats[...] = jnp.sum(row, axis=0, keepdims=True)


def volume_stage(
    depth_total, depth_local, cols, own, left, right, edge, feats, shifts, frame, shift_rows, mat, out,
    pack_left, pack_right, stats, slab
):
    views, high, n = own.shape
    channels = high // ROWS
    first_depth = lax.axis_index("depth") * depth_local
    first_col = lax.axis_index("col") * n
    lane = iota((ROWS, LANES), 1)
    pair_lane = iota((2 * ROWS, LANES), 1)

    def one_depth(step, _):
        depth = first_depth + step - 1
        valid = (depth >= 0) & (depth < depth_total)
        clipped = jnp.clip(depth, 0, depth_total - 1)
        moves = [shifts[v, clipped] for v in range(views)]
        for j in range(n // LANES):
            x = first_col + j * LANES + lane
            wraps = []
            tally = jnp.zeros((ROWS, LANES), f32)
            for v in range(views):
                c = x - moves[v]
                mask = (c >= frame[0, v]) & (c < frame[1, v])
                tally = tally + jnp.where(mask, 1.0, 0.0)
                wraps.append(pair_lane >= LANES - moves[v])
            scale = 1.0 / tally
            last_scale = jnp.where(valid, scale, 0.0)
            scale, last_scale = [
                jnp.concatenate([part, part], axis=0) for part in (scale, last_scale)
            ]

            def one_pair(pair, _):
                rows = pl.ds(pl.multiple_of(pair * 2 * ROWS, 2 * ROWS), 2 * ROWS)
                vals = []
                for v in range(views):
                    value = feats[v, rows, (j + 1) * LANES : (j + 2) * LANES]
                    if v:
                        behind = feats[v, rows, j * LANES : (j + 1) * LANES]
                        value = pltpu.roll(jnp.where(wraps[v], behind, value), moves[v], 1)
                    vals.append(value.astype(f32))
                total = tree_sum(vals)
                square = tree_sum([value * value for value in vals])
                square = jnp.maximum(square - total * (total * scale), 0.0) * last_scale
                where_to = pl.ds(pl.multiple_of(step * high + pair * 2 * ROWS, 2 * ROWS), 2 * ROWS)
                slab[where_to, j * LANES : (j + 1) * LANES] = square.astype(bf16)
                return _

            lax.fori_loop(0, channels // 2, one_pair, 0, unroll=True)
        return _

    lax.fori_loop(0, depth_local + 2, one_depth, 0, unroll=2)

    view_lane = iota(right.shape, 1)
    ahead = jnp.zeros(right.shape, bf16)
    for v in range(views):
        c = first_col + n
        seen = (c >= frame[0, v]) & (c < frame[1, v]) & (view_lane == v)
        ahead = jnp.where(seen, right[...], ahead)
    half = LANES // 2
    padding = jnp.zeros((views, LANES - depth_total), jnp.int32)
    padded = jnp.concatenate([shift_rows[...], padding], axis=1)
    lane_row = iota((1, LANES), 1)
    far = lane_row >= half
    step_row = jnp.where(far, lane_row - half, lane_row)
    depth_row = first_depth + step_row - 1
    lane_shifts = jnp.where(
        far,
        pltpu.roll(padded, lax.rem(LANES + half + 1 - first_depth, LANES), 1),
        pltpu.roll(padded, lax.rem(LANES + 1 - first_depth, LANES), 1),
    )
    x_row = jnp.where(far, first_col + n, first_col - 1)
    row_id = iota((n + LANES, LANES), 0)
    base = jnp.where(far, n + LANES, LANES - 1)
    total = jnp.zeros((high, LANES), f32)
    squares = jnp.zeros((high, LANES), f32)
    tally = jnp.zeros((1, LANES), f32)
    touch = jnp.zeros((LANES, LANES), f32)
    for v in range(views):
        shift_row = lane_shifts[v : v + 1, :]
        pick = row_id == base - shift_row
        found = dot(feats[v], jnp.where(pick, 1.0, 0.0).astype(bf16))
        total = total + found
        squares = squares + found * found
        c = x_row - shift_row
        tally = tally + jnp.where((c >= frame[0, v]) & (c < frame[1, v]), 1.0, 0.0)
        hit = far & (shift_row == 0) & (iota((LANES, LANES), 0) == v)
        touch = jnp.where(hit, 1.0, touch)
    touch = touch.astype(bf16)
    wide = ahead.astype(f32) * ahead.astype(f32)
    coarse = wide.astype(bf16)
    fine = (wide - coarse.astype(f32)).astype(bf16)
    total = total + dot(ahead, touch)
    squares = squares + dot(coarse, touch) + dot(fine, touch)
    scale = 1.0 / jnp.maximum(tally, 1.0)
    keep = (depth_row >= 0) & (depth_row < depth_total) & (step_row < depth_local + 2)
    keep = keep & (x_row >= 0) & (x_row < n * cols)
    square = jnp.maximum(squares - total * (total * scale), 0.0)
    halo = jnp.where(keep, square * scale, 0.0).astype(bf16)
    convolve(
        slab, high, mat, halo, halo, half, mat.shape[0] // 3, depth_local, out, pack_left, pack_right,
        stats
    )


def exchange(
    depths, cols, voxels, conv, pack_left, pack_right, stats, slab, plane_low, plane_high, from_left,
    from_right, others, s_near, r_near, s_all, r_all, known=None
):
    me, col = lax.axis_index("depth"), lax.axis_index("col")
    depth_local, high, n = conv.shape
    has_left, has_right = col > 0, col < cols - 1
    has_low, has_high = me > 0, me < depths - 1
    def to_all(k):
        kd, kc = k // cols, lax.rem(k, cols)
        return remote(
            stats, others.at[k - 1], s_all.at[0], r_all.at[0], lax.rem(me + kd, depths),
            lax.rem(col + kc, cols)
        )

    if known is not None:
        known()
    if depths * cols > 64:
        lax.fori_loop(1, depths * cols, lambda k, _: (to_all(k).start(), _)[1], 0)
    else:
        for k in range(1, depths * cols):
            to_all(jnp.int32(k)).start()
    near = []
    down = lambda: remote(conv.at[0], plane_high, s_near.at[0], r_near.at[0], me - 1, col)
    up = lambda: remote(
        conv.at[depth_local - 1], plane_low, s_near.at[1], r_near.at[1], me + 1, col
    )
    near.append((down, has_low, has_high))
    near.append((up, has_high, has_low))
    always = col >= 0
    for i, (dd, ok, back) in enumerate(
        ((-1, has_low, has_high), (0, always, always), (1, has_high, has_low))
    ):
        near.append(
            (
                lambda dd=dd, i=i: remote(
                    pack_right, from_left.at[1 - dd], s_near.at[2 + i], r_near.at[2 + i], me + dd, col + 1
                ),
                ok & has_right,
                back & has_left,
            )
        )
        near.append(
            (
                lambda dd=dd, i=i: remote(
                    pack_left, from_right.at[1 - dd], s_near.at[5 + i], r_near.at[5 + i], me + dd, col - 1
                ),
                ok & has_left,
                back & has_right,
            )
        )
    for copy, sends, _ in near:
        pl.when(sends)(lambda copy=copy: copy().start())

    for copy, _, receives in near:
        pl.when(receives)(lambda copy=copy: copy().wait_recv())
    everyone = remote(others, others, s_all.at[0], r_all.at[0], me, col)
    everyone.wait_recv()
    count = high // ROWS
    sums = jnp.broadcast_to(jnp.sum(others[...], axis=0) + stats[...], (count, LANES))
    spot = iota((count, LANES), 1) - iota((count, LANES), 0)

    def pick(at):
        return jnp.sum(jnp.where(spot == at, sums, 0.0), axis=1, keepdims=True) / voxels

    average = pick(0)
    variance = pick(count) - average * average
    average = spread_rows(jnp.broadcast_to(average, (high // ROWS, LANES)))
    factor = spread_rows(jnp.broadcast_to(lax.rsqrt(variance + norm_eps), (high // ROWS, LANES)))

    def activate(x):
        return jnp.maximum((x - average) * factor, 0.0)

    def activate_plane(x):
        parts = [activate(x[:, j * LANES : (j + 1) * LANES]) for j in range(n // LANES)]
        return jnp.concatenate(parts, axis=1) if len(parts) > 1 else parts[0]

    slab[0:high, :] = jnp.where(has_low, activate_plane(plane_low[...]), 0.0).astype(bf16)
    slab[(depth_local + 1) * high : (depth_local + 2) * high, :] = jnp.where(
        has_high, activate_plane(plane_high[...]), 0.0
    ).astype(bf16)

    def one_plane(d, _):
        slab[pl.ds(pl.multiple_of((d + 1) * high, high), high), :] = activate_plane(conv[d]).astype(
            bf16
        )
        return _

    lax.fori_loop(0, depth_local, one_plane, 0, unroll=2)
    lane = iota((high, LANES), 1)
    halos = []
    for parts, ok in ((from_left, has_left), (from_right, has_right)):
        low = pltpu.roll(parts[0], LANES - (depth_local - 1), 1)
        mid = pltpu.roll(parts[1], 1, 1)
        top = pltpu.roll(parts[2], depth_local + 1, 1)
        row = jnp.where(lane == 0, low, jnp.where(lane == depth_local + 1, top, mid))
        keep = ok & (lane <= depth_local + 1)
        keep = keep & (has_low | (lane > 0)) & (has_high | (lane < depth_local + 1))
        halos.append(jnp.where(keep, activate(row), 0.0).astype(bf16))

    def finish():
        everyone.wait_send()
        for copy, sends, _ in near:
            pl.when(sends)(lambda copy=copy: copy().wait_send())

    return halos, finish


def score_stage(
    depths, cols, voxels, depth_total, conv, pack_left, pack_right, stats, mat, out, score, parts,
    s_part, r_part, slab, *rest
):
    me, col = lax.axis_index("depth"), lax.axis_index("col")
    depth_local, high, n = conv.shape
    halos, finish = exchange(
        depths, cols, voxels, conv, pack_left, pack_right, stats, slab, *rest
    )
    convolve(slab, high, mat, halos[0], halos[1], 0, ROWS, depth_local, score, None, None, None)
    planes = [score[d] for d in range(depth_local)]
    peak = functools.reduce(jnp.maximum, planes)
    total = jnp.zeros_like(peak)
    weighted = jnp.zeros_like(peak)
    first_depth = me * depth_local
    for d in range(depth_local):
        term = jnp.exp(planes[d] - peak)
        total = total + term
        weighted = weighted + term * ((first_depth + d).astype(f32) / (depth_total - 1))
    parts[me, 0] = peak
    parts[me, 1] = total
    parts[me, 2] = weighted

    def to_depth(k, slot):
        return remote(
            parts.at[slot], parts.at[slot], s_part.at[k], r_part.at[slot], lax.rem(me + k, depths), col
        )

    for k in range(1, depths):
        to_depth(k, me).start()
    for k in range(1, depths):
        to_depth(k, lax.rem(me + k, depths)).wait_recv()
    highest = functools.reduce(jnp.maximum, [parts[p, 0] for p in range(depths)])
    total = jnp.zeros_like(highest)
    weighted = jnp.zeros_like(highest)
    for p in range(depths):
        scale = jnp.exp(parts[p, 0] - highest)
        total = total + parts[p, 1] * scale
        weighted = weighted + parts[p, 2] * scale
    out[...] = weighted / total
    finish()
    for k in range(1, depths):
        to_depth(k, me).wait_send()


def whole_kernel(groups, depths, cols, voxels, depth_total, depth_local, *refs):
    (
        raw_views, feat_weight, cost_weight, mid_weight, final_weight, shifts, frame, shift_rows, out
    ) = refs[:9]
    rest, taken = [], 9
    for size in groups:
        rest.append(refs[taken : taken + size])
        taken += size
    gathered, mats, feature_refs, volume_refs, first, second, swap_a, swap_b, score_refs, known = rest
    known_sem = known[0]
    me, col = lax.axis_index("depth"), lax.axis_index("col")
    has_left, has_right = col > 0, col < cols - 1
    has_low, has_high = me > 0, me < depths - 1
    count = lambda flag: flag.astype(jnp.int32)
    barrier = pltpu.get_barrier_semaphore()

    def greet(d, c):
        pl.semaphore_signal(barrier, inc=1, device_id=(d, c), device_id_type=MESH)

    for k in range(1, depths):
        greet(lax.rem(me + k, depths), col)
    for k in range(1, cols):
        greet(me, lax.rem(col + k, cols))
    for dd, ok_d in ((-1, has_low), (1, has_high)):
        for dc, ok_c in ((-1, has_left), (1, has_right)):
            pl.when(ok_d & ok_c)(lambda dd=dd, dc=dc: greet(me + dd, col + dc))
    diagonals = (count(has_low) + count(has_high)) * (count(has_left) + count(has_right))

    def ready():
        pl.semaphore_wait(barrier, depths - 1 + cols - 1 + diagonals)
        for k in range(1, cols):
            pl.semaphore_signal(
                known_sem, inc=1, device_id=(me, lax.rem(col + k, cols)), device_id_type=MESH
            )

    def all_known():
        pl.semaphore_wait(known_sem, cols - 1)

    sent = feature_stage(
        depths, cols, ready, raw_views, feat_weight, cost_weight, mid_weight, final_weight, frame,
        *gathered, *mats, *feature_refs
    )
    volume_stage(
        depth_total, depth_local, cols, *gathered, shifts, frame, shift_rows, mats[0], *first,
        *volume_refs
    )
    halos, finish = exchange(depths, cols, voxels, *first, *swap_a, all_known)
    high = first[0].shape[1]
    convolve(swap_a[0], high, mats[1], halos[0], halos[1], 0, high, depth_local, *second)
    finish()
    sent()
    score_stage(depths, cols, voxels, depth_total, *second, mats[2], out, *score_refs, *swap_b)


def buffer(dims, kind):
    return pltpu.VMEM(dims, kind)


def dma(n):
    return pltpu.SemaphoreType.DMA((n,))


def local(raw_views, feat_weight, shifts, frame_range, cost_weight, mid_weight, final_weight):
    view_local, channels, rows, n = raw_views.shape
    depths, cols = lax.axis_size("depth"), lax.axis_size("col")
    views, depth_total = shifts.shape
    depth_local = depth_total // depths
    high = channels * rows
    hidden = cost_weight.shape[1]
    mid_high = hidden * rows
    voxels = float(depth_total * rows * n * cols)

    gathered = [
        buffer((views, high, n), bf16),
        buffer((views, high, LANES), bf16),
        buffer((high, LANES), bf16),
        buffer((high, LANES), bf16),
        buffer((views, high, n + LANES), bf16),
    ]
    mats = [
        buffer((3 * mid_high, 3 * high), bf16),
        buffer((3 * mid_high, 3 * mid_high), bf16),
        buffer((3 * rows, 3 * mid_high), bf16),
    ]
    feature_refs = [
        buffer((view_local, high, n), bf16),
        buffer((9, channels, high), f32),
        buffer((27, hidden, high), f32),
        buffer((hidden, 27, mid_high), f32),
        buffer((1, 27, mid_high), f32),
        buffer((high, LANES), bf16),
        buffer((high, LANES), bf16),
        buffer((high, LANES), bf16),
        buffer((view_local, high, n), f32),
        buffer((3 * high, high), bf16),
        dma(2), dma(2), dma(views), dma(views), dma(views), dma(views), dma(1), dma(1),
    ]
    volume_refs = [
        buffer(((depth_local + 2) * high, n), bf16),
    ]

    def conv_refs():
        return [
            buffer((depth_local, mid_high, n), f32),
            buffer((mid_high, LANES), f32),
            buffer((mid_high, LANES), f32),
            buffer((1, LANES), f32),
        ]

    def swap_refs():
        return [
            buffer(((depth_local + 2) * mid_high, n), bf16),
            buffer((mid_high, n), f32),
            buffer((mid_high, n), f32),
            buffer((3, mid_high, LANES), f32),
            buffer((3, mid_high, LANES), f32),
            buffer((depths * cols - 1, 1, LANES), f32),
            dma(8), dma(8), dma(1), dma(1),
        ]

    score_refs = [
        buffer((depth_local, rows, n), f32),
        buffer((depths, 3, rows, n), f32),
        dma(depths), dma(depths),
    ]
    groups = [
        gathered, mats, feature_refs, volume_refs, conv_refs(), conv_refs(), swap_refs(), swap_refs(),
        score_refs, [pltpu.SemaphoreType.REGULAR],
    ]
    return pl.pallas_call(
        functools.partial(
            whole_kernel, [len(g) for g in groups], depths, cols, voxels, depth_total, depth_local
        ),
        out_shape=jax.ShapeDtypeStruct((rows, n), f32),
        in_specs=[vmem] * 5 + [smem] * 2 + [vmem],
        out_specs=vmem,
        scratch_shapes=[ref for g in groups for ref in g],
        compiler_params=pltpu.CompilerParams(collective_id=0, has_side_effects=True),
        name="whole",
    )(
        raw_views, feat_weight, cost_weight, jnp.transpose(mid_weight, (1, 2, 0)),
        jnp.transpose(final_weight)[None], shifts, jnp.transpose(frame_range), shifts
    )


def solution(mesh):
    in_specs = (P("depth", None, None, "col"), P(), P(), P(), P(), P(), P())
    out_specs = P(None, "col")
    return jax.shard_map(local, mesh=mesh, in_specs=in_specs, out_specs=out_specs, check_vma=False)
```

```python
import functools
import jax
import jax.numpy as jnp
from jax import lax
from jax.experimental import pallas as pl
from jax.experimental.pallas import tpu as pltpu
from jax.sharding import PartitionSpec as P

norm_eps = 1e-05
LANES = 128
ROWS = 8
f32 = jnp.float32
bf16 = jnp.bfloat16
MESH = pl.DeviceIdType.MESH
vmem = pl.BlockSpec(memory_space=pltpu.VMEM)
smem = pl.BlockSpec(memory_space=pltpu.SMEM)


def dot(a, b):
    return jnp.dot(a, b, preferred_element_type=f32)


def iota(shape, dim):
    return lax.broadcasted_iota(jnp.int32, shape, dim)


def remote(src, dst, send, recv, depth, col):
    return pltpu.make_async_remote_copy(
        src_ref=src,
        dst_ref=dst,
        send_sem=send,
        recv_sem=recv,
        device_id=(depth, col),
        device_id_type=MESH,
    )


def tree_sum(parts):
    while len(parts) > 1:
        paired = [a + b for a, b in zip(parts[::2], parts[1::2])]
        parts = paired + parts[len(paired) * 2 :]
    return parts[0]


def spread_rows(table):
    pieces = [
        jnp.broadcast_to(table[o : o + 1], (ROWS, table.shape[1])) for o in range(table.shape[0])
    ]
    return jnp.concatenate(pieces, axis=0)


def expand(weight_ref, table_ref, taps_last):
    wide = table_ref.shape[-1]
    spread = iota((wide // ROWS, wide), 1) // ROWS == iota((wide // ROWS, wide), 0)
    spread = jnp.where(spread, 1.0, 0.0).astype(bf16)
    if taps_last:
        for o in range(weight_ref.shape[0]):
            table_ref[o] = lax.dot_general(
                weight_ref[o], spread, (((0,), (0,)), ((), ())), preferred_element_type=f32
            )
        return
    for tap in range(weight_ref.shape[0]):
        table_ref[tap] = dot(weight_ref[tap], spread)


def row_bands(width):
    out_row = iota((ROWS, width), 0)
    in_row = lax.rem(iota((ROWS, width), 1), ROWS)
    return [in_row - out_row + 1 == b for b in range(3)]


def banded(table_ref, count, first, step, bands, taps_last):
    pieces = []
    for o in range(count):
        block = jnp.zeros(bands[0].shape, f32)
        for b in range(3):
            tap = first + step * b
            row = table_ref[o, tap : tap + 1, :] if taps_last else table_ref[tap, o : o + 1, :]
            block = jnp.where(bands[b], jnp.broadcast_to(row, block.shape), block)
        pieces.append(block)
    return jnp.concatenate(pieces, axis=0) if count > 1 else pieces[0]


def build_conv(table_ref, count, wide, mat_ref, taps_last):
    bands = row_bands(wide)
    high = count * ROWS
    for a in range(3):
        for e in range(3):
            block = banded(table_ref, count, 9 * a + e, 3, bands, taps_last)
            mat_ref[e * high : (e + 1) * high, a * wide : (a + 1) * wide] = block.astype(
                mat_ref.dtype
            )


def partner(me, depths, k):
    if depths == 4:
        return [me, me + 1 - 2 * lax.rem(me, 2), lax.rem(me + 2, 4), 3 - me][k]
    return lax.rem(me + k, depths)


def origin(me, depths, k):
    return partner(me, depths, k if depths == 4 else (depths - k) % depths)


def feature_stage(
    depths, cols, ready, run_pass, raw_views, feat_weight, cost_weight, mid_weight, final_weight, frame, own, left,
    right, edge, feats, cost_mat, mid_mat, final_mat, raw, table, cost_table, mid_table, final_table,
    rim, rim_left, rim_right, partial, mat, s_raw, r_raw, s_dep, r_dep, s_right, r_right, s_left, r_left
):
    me, col = lax.axis_index("depth"), lax.axis_index("col")
    count, high, n = raw.shape
    views = depths * count
    channels = high // ROWS
    has_left, has_right = col > 0, col < cols - 1
    first_col = col * n
    lane = iota((high, LANES), 1)
    half = LANES // 2
    raw[...] = raw_views[...].reshape(raw.shape)
    packed = jnp.zeros((high, LANES), bf16)
    for v in range(count):
        first, last = raw[v, :, 0:LANES], raw[v, :, n - LANES : n]
        packed = jnp.where(lane == v, pltpu.roll(first, v, 1) if v else first, packed)
        packed = jnp.where(lane == half + v, pltpu.roll(last, half + v + 1, 1), packed)
    rim[...] = packed
    ready()

    def edge_right():
        return remote(rim, rim_left, s_raw.at[0], r_raw.at[0], me, col + 1)

    def edge_left():
        return remote(rim, rim_right, s_raw.at[1], r_raw.at[1], me, col - 1)

    pl.when(has_right)(lambda: edge_right().start())
    pl.when(has_left)(lambda: edge_left().start())
    expand(feat_weight, table, False)
    bands = row_bands(high)
    for e in range(3):
        mat[e * high : (e + 1) * high, :] = banded(
            table, channels, e, 3, bands, False
        ).astype(bf16)
    column = iota((high, n), 1)
    for v in range(count):
        before = pltpu.roll(dot(mat[0:high, :], raw[v]), 1, 1)
        after = pltpu.roll(dot(mat[2 * high : 3 * high, :], raw[v]), n - 1, 1)
        total = jnp.where(column == 0, 0.0, before) + dot(mat[high : 2 * high, :], raw[v])
        partial[v] = total + jnp.where(column == n - 1, 0.0, after)
    pl.when(has_left)(lambda: edge_right().wait_recv())
    pl.when(has_right)(lambda: edge_left().wait_recv())
    pick = has_left & (lane >= half) & (lane < half + count)
    before = dot(mat[0:high, :], jnp.where(pick, rim_left[...].astype(f32), 0.0).astype(bf16))
    pick = has_right & (lane < count)
    after = dot(
        mat[2 * high : 3 * high, :], jnp.where(pick, rim_right[...].astype(f32), 0.0).astype(bf16)
    )
    zero = jnp.zeros((high, n - LANES), f32)
    for v in range(count):
        low = jnp.where(lane == 0, pltpu.roll(before, half - v, 1), 0.0)
        top = jnp.where(lane == LANES - 1, pltpu.roll(after, LANES - 1 - v, 1), 0.0)
        if n > LANES:
            low = jnp.concatenate([low, zero], axis=1)
            top = jnp.concatenate([zero, top], axis=1)
        own[me * count + v] = (partial[v] + low + top).astype(bf16)

    relayed = depths == 4 and count == 2
    at = [[origin(me, depths, k) * count + j for j in range(count)] for k in range(depths)]
    if relayed:
        groups = [[(0, 0), (0, 1)], [(1, 1), (2, 0)], [(1, 0), (2, 1)], [(3, 0), (3, 1)]]
        direct = [(1, 1), (2, 0), (1, 0), (2, 1)]
        relays = {(1, 1): 2, (2, 0): 1}
    else:
        groups = [[(k, j) for j in range(count)] for k in range(depths)]
        direct = [(k, j) for k in range(1, depths) for j in range(count)]
        relays = {}

    def send(v, k, sem):
        return remote(own.at[v], own.at[v], s_dep.at[sem], r_dep.at[v], partner(me, depths, k), col)

    def relay(k, j):
        return send(at[k][j], relays[k, j], depths * count + relays[k, j])

    def to_depth(k, j):
        return send(me * count + j, k, k * count + j)

    def to_right(v):
        return remote(
            own.at[v, :, n - LANES : n], left.at[v], s_right.at[v], r_right.at[v], me, col + 1
        )

    def to_left():
        return remote(edge, right, s_left.at[0], r_left.at[0], me, col - 1)

    for k, j in direct:
        to_depth(k, j).start()
    for j in range(count):
        pl.when(has_right)(lambda j=j: to_right(me * count + j).start())
    for weight, spread, built, taps_last in (
        (cost_weight, cost_table, cost_mat, False),
        (mid_weight, mid_table, mid_mat, True),
        (final_weight, final_table, final_mat, True),
    ):
        expand(weight, spread, taps_last)
        build_conv(spread, built.shape[0] // (3 * ROWS), built.shape[1] // 3, built, taps_last)

    def absorb(v, source, begin, width):
        c = first_col - LANES + begin + iota((high, width), 1)
        seen = (c >= frame[0, v]) & (c < frame[1, v])
        feats[v, :, begin : begin + width] = jnp.where(seen, source[v], jnp.zeros((high, width), bf16))

    def take(group):
        for k, j in group:
            v = at[k][j]
            if k:
                remote(own.at[v], own.at[v], s_dep.at[0], r_dep.at[v], me, col).wait_recv()
                if (k, j) in relays:
                    relay(k, j).start()
                pl.when(has_right)(lambda v=v: to_right(v).start())
        for k, j in group:
            absorb(at[k][j], own, LANES, n)

    def use(index):
        for k, j in groups[index]:
            v = at[k][j]
            pl.when(has_left)(lambda v=v: to_right(v).wait_recv())
            absorb(v, left, 0, LANES)
        run_pass([at[k][j] for k, j in groups[index]], index == 0, index == len(groups) - 1)

    take(groups[0])
    take(groups[1])
    use(0)
    for group in groups[2:]:
        take(group)
    packed = jnp.zeros((high, LANES), bf16)
    for v in range(views):
        first = own[v, :, 0:LANES]
        packed = jnp.where(lane == v, pltpu.roll(first, v, 1) if v else first, packed)
    edge[...] = packed
    pl.when(has_left)(lambda: to_left().start())
    for index in range(1, len(groups)):
        use(index)
    pl.when(has_right)(lambda: to_left().wait_recv())

    def finish():
        pl.when(has_right)(lambda: edge_right().wait_send())
        pl.when(has_left)(lambda: edge_left().wait_send())
        for k, j in direct:
            to_depth(k, j).wait_send()
        for k, j in relays:
            relay(k, j).wait_send()
        for v in range(views):
            pl.when(has_right)(lambda v=v: to_right(v).wait_send())
        pl.when(has_left)(lambda: to_left().wait_send())

    return finish


def convolve(slab, wide, mat, halo_left, halo_right, far, high, depth_local, out, pack_left, pack_right,
             stats):
    n = slab.shape[1]
    tiles = n // LANES
    edge_left = edge_right = None
    for a in range(3):
        w_a = mat[0:high, a * wide : (a + 1) * wide]
        w_b = mat[2 * high : 3 * high, a * wide : (a + 1) * wide]
        part_a = pltpu.roll(dot(w_a, halo_left), (LANES - a) % LANES, 1)
        part_b = pltpu.roll(dot(w_b, halo_right), (LANES - a - far) % LANES, 1)
        edge_left = part_a if edge_left is None else edge_left + part_a
        edge_right = part_b if edge_right is None else edge_right + part_b
    lane = iota((high, LANES), 1)
    column = iota((high, n), 1)
    half = depth_local // 2
    weights = mat[...]

    def over_tiles(x):
        return jnp.concatenate([x] * tiles, axis=1) if tiles > 1 else x

    def one_step(t, carry):
        halves = []
        for g in range(2):
            start = pl.multiple_of((t + g * half) * wide, wide)
            halves.append(slab[pl.ds(start, 3 * wide), :])
        product = dot(weights, jnp.concatenate(halves, axis=1))
        carry = list(carry)
        for g in range(2):
            d = t + g * half
            part = product[:, g * n : (g + 1) * n]
            from_left = pltpu.roll(part[0:high], 1, 1)
            from_right = pltpu.roll(part[2 * high : 3 * high], n - 1, 1)
            rim_left = over_tiles(pltpu.roll(edge_left, lax.rem(LANES - d, LANES), 1))
            rim_right = over_tiles(pltpu.roll(edge_right, LANES - 1 - d, 1))
            result = (
                jnp.where(column == 0, rim_left, from_left)
                + part[high : 2 * high]
                + jnp.where(column == n - 1, rim_right, from_right)
            )
            out[d] = result
            if stats is not None:
                carry[0] = carry[0] + result
                carry[1] = carry[1] + result * result
                carry[2] = jnp.where(lane == d, pltpu.roll(result[:, 0:LANES], d, 1), carry[2])
                carry[3] = jnp.where(
                    lane == d, pltpu.roll(result[:, n - LANES : n], d + 1, 1), carry[3]
                )
        return tuple(carry)

    if stats is None:
        lax.fori_loop(0, half, one_step, (), unroll=4)
        return
    wide_zero = jnp.zeros((high, n), f32)
    lane_zero = jnp.zeros((high, LANES), f32)
    first, second, pack_l, pack_r = lax.fori_loop(
        0, half, one_step, (wide_zero, wide_zero, lane_zero, lane_zero), unroll=2
    )
    pack_left[...] = pack_l
    pack_right[...] = pack_r

    def per_channel(x):
        x = sum(x[:, j * LANES : (j + 1) * LANES] for j in range(tiles))
        rows = [
            jnp.sum(x[o * ROWS : (o + 1) * ROWS], axis=0, keepdims=True)
            for o in range(high // ROWS)
        ]
        return jnp.concatenate(rows, axis=0)

    count = high // ROWS
    spot = iota((count, LANES), 1) - iota((count, LANES), 0)
    total = jnp.sum(per_channel(first), axis=1, keepdims=True)
    squares = jnp.sum(per_channel(second), axis=1, keepdims=True)
    row = jnp.where(spot == 0, total, jnp.where(spot == count, squares, 0.0))
    stats[...] = jnp.sum(row, axis=0, keepdims=True)


def volume_pass(
    depth_total, depth_local, picked, first, last, feats, shifts, frame, slab, sum_one, sum_two
):
    views, high, n = feats.shape
    n = n - LANES
    channels = high // ROWS
    first_depth = lax.axis_index("depth") * depth_local
    first_col = lax.axis_index("col") * n
    lane = iota((ROWS, LANES), 1)
    pair_lane = iota((2 * ROWS, LANES), 1)

    def one_depth(step, _):
        depth = first_depth + step - 1
        valid = (depth >= 0) & (depth < depth_total)
        clipped = jnp.clip(depth, 0, depth_total - 1)
        moves = [shifts[v, clipped] for v in picked]
        wraps = [pair_lane >= LANES - move for move in moves]
        for j in range(n // LANES):
            here = slice(j * LANES, (j + 1) * LANES)
            if last:
                x = first_col + j * LANES + lane
                tally = jnp.zeros((ROWS, LANES), f32)
                for v in range(views):
                    c = x - shifts[v, clipped]
                    mask = (c >= frame[0, v]) & (c < frame[1, v])
                    tally = tally + jnp.where(mask, 1.0, 0.0)
                scale = 1.0 / tally
                last_scale = jnp.where(valid, scale, 0.0)
                scale, last_scale = [
                    jnp.concatenate([part, part], axis=0) for part in (scale, last_scale)
                ]
            for pair in range(channels // 2):
                rows = slice(pair * 2 * ROWS, (pair + 1) * 2 * ROWS)
                where_to = pl.ds(pl.multiple_of(step * high + pair * 2 * ROWS, 2 * ROWS), 2 * ROWS)
                ones, twos = [], []
                if not first:
                    ones.append(sum_one[where_to, here])
                    twos.append(sum_two[where_to, here])
                for v, move, wrap in zip(picked, moves, wraps):
                    value = feats[v, rows, (j + 1) * LANES : (j + 2) * LANES]
                    behind = feats[v, rows, here]
                    value = pltpu.roll(jnp.where(wrap, behind, value), move, 1).astype(f32)
                    ones.append(value)
                    twos.append(value * value)
                total, square = tree_sum(ones), tree_sum(twos)
                if last:
                    square = jnp.maximum(square - total * (total * scale), 0.0) * last_scale
                    slab[where_to, here] = square.astype(bf16)
                else:
                    sum_one[where_to, here] = total
                    sum_two[where_to, here] = square
        return _

    lax.fori_loop(0, depth_local + 2, one_depth, 0, unroll=2)


def volume_stage(
    depth_total, depth_local, cols, own, left, right, edge, feats, shifts, frame, shift_rows, mat, out,
    pack_left, pack_right, stats, slab, sum_one, sum_two
):
    views, high, n = own.shape
    channels = high // ROWS
    first_depth = lax.axis_index("depth") * depth_local
    first_col = lax.axis_index("col") * n
    view_lane = iota(right.shape, 1)
    ahead = jnp.zeros(right.shape, bf16)
    for v in range(views):
        c = first_col + n
        seen = (c >= frame[0, v]) & (c < frame[1, v]) & (view_lane == v)
        ahead = jnp.where(seen, right[...], ahead)
    half = LANES // 2
    padding = jnp.zeros((views, LANES - depth_total), jnp.int32)
    padded = jnp.concatenate([shift_rows[...], padding], axis=1)
    lane_row = iota((1, LANES), 1)
    far = lane_row >= half
    step_row = jnp.where(far, lane_row - half, lane_row)
    depth_row = first_depth + step_row - 1
    lane_shifts = jnp.where(
        far,
        pltpu.roll(padded, lax.rem(LANES + half + 1 - first_depth, LANES), 1),
        pltpu.roll(padded, lax.rem(LANES + 1 - first_depth, LANES), 1),
    )
    x_row = jnp.where(far, first_col + n, first_col - 1)
    row_id = iota((n + LANES, LANES), 0)
    base = jnp.where(far, n + LANES, LANES - 1)
    total = jnp.zeros((high, LANES), f32)
    squares = jnp.zeros((high, LANES), f32)
    tally = jnp.zeros((1, LANES), f32)
    touch = jnp.zeros((LANES, LANES), f32)
    for v in range(views):
        shift_row = lane_shifts[v : v + 1, :]
        pick = row_id == base - shift_row
        found = dot(feats[v], jnp.where(pick, 1.0, 0.0).astype(bf16))
        total = total + found
        squares = squares + found * found
        c = x_row - shift_row
        tally = tally + jnp.where((c >= frame[0, v]) & (c < frame[1, v]), 1.0, 0.0)
        hit = far & (shift_row == 0) & (iota((LANES, LANES), 0) == v)
        touch = jnp.where(hit, 1.0, touch)
    touch = touch.astype(bf16)
    wide = ahead.astype(f32) * ahead.astype(f32)
    coarse = wide.astype(bf16)
    fine = (wide - coarse.astype(f32)).astype(bf16)
    total = total + dot(ahead, touch)
    squares = squares + dot(coarse, touch) + dot(fine, touch)
    scale = 1.0 / jnp.maximum(tally, 1.0)
    keep = (depth_row >= 0) & (depth_row < depth_total) & (step_row < depth_local + 2)
    keep = keep & (x_row >= 0) & (x_row < n * cols)
    square = jnp.maximum(squares - total * (total * scale), 0.0)
    halo = jnp.where(keep, square * scale, 0.0).astype(bf16)
    convolve(
        slab, high, mat, halo, halo, half, mat.shape[0] // 3, depth_local, out, pack_left, pack_right,
        stats
    )


def exchange(
    depths, cols, voxels, conv, pack_left, pack_right, stats, slab, plane_low, plane_high, from_left,
    from_right, others, s_near, r_near, s_all, r_all, known=None
):
    me, col = lax.axis_index("depth"), lax.axis_index("col")
    depth_local, high, n = conv.shape
    has_left, has_right = col > 0, col < cols - 1
    has_low, has_high = me > 0, me < depths - 1
    def to_all(k):
        kd, kc = k // cols, lax.rem(k, cols)
        return remote(
            stats, others.at[k - 1], s_all.at[0], r_all.at[0], lax.rem(me + kd, depths),
            lax.rem(col + kc, cols)
        )

    if known is not None:
        known()
    if depths * cols > 64:
        lax.fori_loop(1, depths * cols, lambda k, _: (to_all(k).start(), _)[1], 0)
    else:
        for k in range(1, depths * cols):
            to_all(jnp.int32(k)).start()
    near = []
    down = lambda: remote(conv.at[0], plane_high, s_near.at[0], r_near.at[0], me - 1, col)
    up = lambda: remote(
        conv.at[depth_local - 1], plane_low, s_near.at[1], r_near.at[1], me + 1, col
    )
    near.append((down, has_low, has_high))
    near.append((up, has_high, has_low))
    always = col >= 0
    for i, (dd, ok, back) in enumerate(
        ((-1, has_low, has_high), (0, always, always), (1, has_high, has_low))
    ):
        near.append(
            (
                lambda dd=dd, i=i: remote(
                    pack_right, from_left.at[1 - dd], s_near.at[2 + i], r_near.at[2 + i], me + dd, col + 1
                ),
                ok & has_right,
                back & has_left,
            )
        )
        near.append(
            (
                lambda dd=dd, i=i: remote(
                    pack_left, from_right.at[1 - dd], s_near.at[5 + i], r_near.at[5 + i], me + dd, col - 1
                ),
                ok & has_left,
                back & has_right,
            )
        )
    for copy, sends, _ in near:
        pl.when(sends)(lambda copy=copy: copy().start())

    for copy, _, receives in near:
        pl.when(receives)(lambda copy=copy: copy().wait_recv())
    everyone = remote(others, others, s_all.at[0], r_all.at[0], me, col)
    everyone.wait_recv()
    count = high // ROWS
    sums = jnp.broadcast_to(jnp.sum(others[...], axis=0) + stats[...], (count, LANES))
    spot = iota((count, LANES), 1) - iota((count, LANES), 0)

    def pick(at):
        return jnp.sum(jnp.where(spot == at, sums, 0.0), axis=1, keepdims=True) / voxels

    average = pick(0)
    variance = pick(count) - average * average
    average = spread_rows(jnp.broadcast_to(average, (high // ROWS, LANES)))
    factor = spread_rows(jnp.broadcast_to(lax.rsqrt(variance + norm_eps), (high // ROWS, LANES)))

    def activate(x):
        return jnp.maximum((x - average) * factor, 0.0)

    def activate_plane(x):
        parts = [activate(x[:, j * LANES : (j + 1) * LANES]) for j in range(n // LANES)]
        return jnp.concatenate(parts, axis=1) if len(parts) > 1 else parts[0]

    slab[0:high, :] = jnp.where(has_low, activate_plane(plane_low[...]), 0.0).astype(bf16)
    slab[(depth_local + 1) * high : (depth_local + 2) * high, :] = jnp.where(
        has_high, activate_plane(plane_high[...]), 0.0
    ).astype(bf16)

    def one_plane(d, _):
        slab[pl.ds(pl.multiple_of((d + 1) * high, high), high), :] = activate_plane(conv[d]).astype(
            bf16
        )
        return _

    lax.fori_loop(0, depth_local, one_plane, 0, unroll=2)
    lane = iota((high, LANES), 1)
    halos = []
    for parts, ok in ((from_left, has_left), (from_right, has_right)):
        low = pltpu.roll(parts[0], LANES - (depth_local - 1), 1)
        mid = pltpu.roll(parts[1], 1, 1)
        top = pltpu.roll(parts[2], depth_local + 1, 1)
        row = jnp.where(lane == 0, low, jnp.where(lane == depth_local + 1, top, mid))
        keep = ok & (lane <= depth_local + 1)
        keep = keep & (has_low | (lane > 0)) & (has_high | (lane < depth_local + 1))
        halos.append(jnp.where(keep, activate(row), 0.0).astype(bf16))

    def finish():
        everyone.wait_send()
        for copy, sends, _ in near:
            pl.when(sends)(lambda copy=copy: copy().wait_send())

    return halos, finish


def score_stage(
    depths, cols, voxels, depth_total, conv, pack_left, pack_right, stats, mat, out, score, parts,
    s_part, r_part, slab, *rest
):
    me, col = lax.axis_index("depth"), lax.axis_index("col")
    depth_local, high, n = conv.shape
    halos, finish = exchange(
        depths, cols, voxels, conv, pack_left, pack_right, stats, slab, *rest
    )
    convolve(slab, high, mat, halos[0], halos[1], 0, ROWS, depth_local, score, None, None, None)
    planes = [score[d] for d in range(depth_local)]
    peak = functools.reduce(jnp.maximum, planes)
    total = jnp.zeros_like(peak)
    weighted = jnp.zeros_like(peak)
    first_depth = me * depth_local
    for d in range(depth_local):
        term = jnp.exp(planes[d] - peak)
        total = total + term
        weighted = weighted + term * ((first_depth + d).astype(f32) / (depth_total - 1))
    parts[me, 0] = peak
    parts[me, 1] = total
    parts[me, 2] = weighted

    def to_depth(k, slot):
        return remote(
            parts.at[slot], parts.at[slot], s_part.at[k], r_part.at[slot], lax.rem(me + k, depths), col
        )

    for k in range(1, depths):
        to_depth(k, me).start()
    for k in range(1, depths):
        to_depth(k, lax.rem(me + k, depths)).wait_recv()
    highest = functools.reduce(jnp.maximum, [parts[p, 0] for p in range(depths)])
    total = jnp.zeros_like(highest)
    weighted = jnp.zeros_like(highest)
    for p in range(depths):
        scale = jnp.exp(parts[p, 0] - highest)
        total = total + parts[p, 1] * scale
        weighted = weighted + parts[p, 2] * scale
    out[...] = weighted / total
    finish()
    for k in range(1, depths):
        to_depth(k, me).wait_send()


def whole_kernel(groups, depths, cols, voxels, depth_total, depth_local, *refs):
    (
        raw_views, feat_weight, cost_weight, mid_weight, final_weight, shifts, frame, shift_rows, out
    ) = refs[:9]
    rest, taken = [], 9
    for size in groups:
        rest.append(refs[taken : taken + size])
        taken += size
    gathered, mats, feature_refs, volume_refs, first, second, swap_a, swap_b, score_refs, known = rest
    known_sem = known[0]
    me, col = lax.axis_index("depth"), lax.axis_index("col")
    has_left, has_right = col > 0, col < cols - 1
    has_low, has_high = me > 0, me < depths - 1
    count = lambda flag: flag.astype(jnp.int32)
    barrier = pltpu.get_barrier_semaphore()

    def greet(d, c):
        pl.semaphore_signal(barrier, inc=1, device_id=(d, c), device_id_type=MESH)

    for k in range(1, depths):
        greet(lax.rem(me + k, depths), col)
    for k in range(1, cols):
        greet(me, lax.rem(col + k, cols))
    for dd, ok_d in ((-1, has_low), (1, has_high)):
        for dc, ok_c in ((-1, has_left), (1, has_right)):
            pl.when(ok_d & ok_c)(lambda dd=dd, dc=dc: greet(me + dd, col + dc))
    diagonals = (count(has_low) + count(has_high)) * (count(has_left) + count(has_right))

    def ready():
        pl.semaphore_wait(barrier, depths - 1 + cols - 1 + diagonals)
        for k in range(1, cols):
            pl.semaphore_signal(
                known_sem, inc=1, device_id=(me, lax.rem(col + k, cols)), device_id_type=MESH
            )

    def all_known():
        pl.semaphore_wait(known_sem, cols - 1)

    feats = gathered[4]

    def run_pass(picked, first_pass, last_pass):
        volume_pass(
            depth_total, depth_local, picked, first_pass, last_pass, feats, shifts, frame, *volume_refs
        )

    sent = feature_stage(
        depths, cols, ready, run_pass, raw_views, feat_weight, cost_weight, mid_weight, final_weight, frame,
        *gathered, *mats, *feature_refs
    )
    volume_stage(
        depth_total, depth_local, cols, *gathered, shifts, frame, shift_rows, mats[0], *first,
        *volume_refs
    )
    halos, finish = exchange(depths, cols, voxels, *first, *swap_a, all_known)
    high = first[0].shape[1]
    convolve(swap_a[0], high, mats[1], halos[0], halos[1], 0, high, depth_local, *second)
    finish()
    sent()
    score_stage(depths, cols, voxels, depth_total, *second, mats[2], out, *score_refs, *swap_b)


def buffer(dims, kind):
    return pltpu.VMEM(dims, kind)


def dma(n):
    return pltpu.SemaphoreType.DMA((n,))


def local(raw_views, feat_weight, shifts, frame_range, cost_weight, mid_weight, final_weight):
    view_local, channels, rows, n = raw_views.shape
    depths, cols = lax.axis_size("depth"), lax.axis_size("col")
    views, depth_total = shifts.shape
    depth_local = depth_total // depths
    high = channels * rows
    hidden = cost_weight.shape[1]
    mid_high = hidden * rows
    voxels = float(depth_total * rows * n * cols)

    gathered = [
        buffer((views, high, n), bf16),
        buffer((views, high, LANES), bf16),
        buffer((high, LANES), bf16),
        buffer((high, LANES), bf16),
        buffer((views, high, n + LANES), bf16),
    ]
    mats = [
        buffer((3 * mid_high, 3 * high), bf16),
        buffer((3 * mid_high, 3 * mid_high), bf16),
        buffer((3 * rows, 3 * mid_high), bf16),
    ]
    feature_refs = [
        buffer((view_local, high, n), bf16),
        buffer((9, channels, high), f32),
        buffer((27, hidden, high), f32),
        buffer((hidden, 27, mid_high), f32),
        buffer((1, 27, mid_high), f32),
        buffer((high, LANES), bf16),
        buffer((high, LANES), bf16),
        buffer((high, LANES), bf16),
        buffer((view_local, high, n), f32),
        buffer((3 * high, high), bf16),
        dma(2), dma(2), dma(views + depths), dma(views), dma(views), dma(views), dma(1), dma(1),
    ]
    volume_refs = [
        buffer(((depth_local + 2) * high, n), bf16),
        buffer(((depth_local + 2) * high, n), f32),
        buffer(((depth_local + 2) * high, n), f32),
    ]

    def conv_refs():
        return [
            buffer((depth_local, mid_high, n), f32),
            buffer((mid_high, LANES), f32),
            buffer((mid_high, LANES), f32),
            buffer((1, LANES), f32),
        ]

    def swap_refs():
        return [
            buffer(((depth_local + 2) * mid_high, n), bf16),
            buffer((mid_high, n), f32),
            buffer((mid_high, n), f32),
            buffer((3, mid_high, LANES), f32),
            buffer((3, mid_high, LANES), f32),
            buffer((depths * cols - 1, 1, LANES), f32),
            dma(8), dma(8), dma(1), dma(1),
        ]

    score_refs = [
        buffer((depth_local, rows, n), f32),
        buffer((depths, 3, rows, n), f32),
        dma(depths), dma(depths),
    ]
    groups = [
        gathered, mats, feature_refs, volume_refs, conv_refs(), conv_refs(), swap_refs(), swap_refs(),
        score_refs, [pltpu.SemaphoreType.REGULAR],
    ]
    return pl.pallas_call(
        functools.partial(
            whole_kernel, [len(g) for g in groups], depths, cols, voxels, depth_total, depth_local
        ),
        out_shape=jax.ShapeDtypeStruct((rows, n), f32),
        in_specs=[vmem] * 5 + [smem] * 2 + [vmem],
        out_specs=vmem,
        scratch_shapes=[ref for g in groups for ref in g],
        compiler_params=pltpu.CompilerParams(collective_id=0, has_side_effects=True, vmem_limit_bytes=40 * 2**20),
        name="whole",
    )(
        raw_views, feat_weight, cost_weight, jnp.transpose(mid_weight, (1, 2, 0)),
        jnp.transpose(final_weight)[None], shifts, jnp.transpose(frame_range), shifts
    )


def solution(mesh):
    in_specs = (P("depth", None, None, "col"), P(), P(), P(), P(), P(), P())
    out_specs = P(None, "col")
    return jax.shard_map(local, mesh=mesh, in_specs=in_specs, out_specs=out_specs, check_vma=False)
```

```python
import functools
import jax
import jax.numpy as jnp
from jax import lax
from jax.experimental import pallas as pl
from jax.experimental.pallas import tpu as pltpu
from jax.sharding import PartitionSpec as P

norm_eps = 1e-05
LANES = 128
ROWS = 8
f32 = jnp.float32
bf16 = jnp.bfloat16
MESH = pl.DeviceIdType.MESH
vmem = pl.BlockSpec(memory_space=pltpu.VMEM)
hbm = pl.BlockSpec(memory_space=pltpu.HBM)


def dot(a, b):
    return jnp.dot(a, b, preferred_element_type=f32)


def iota(shape, dim):
    return lax.broadcasted_iota(jnp.int32, shape, dim)


def remote(src, dst, send, recv, depth, col):
    return pltpu.make_async_remote_copy(
        src_ref=src,
        dst_ref=dst,
        send_sem=send,
        recv_sem=recv,
        device_id=(depth, col),
        device_id_type=MESH,
    )


def tree_sum(parts):
    while len(parts) > 1:
        paired = [a + b for a, b in zip(parts[::2], parts[1::2])]
        parts = paired + parts[len(paired) * 2 :]
    return parts[0]


def spread_rows(table):
    pieces = [
        jnp.broadcast_to(table[o : o + 1], (ROWS, table.shape[1])) for o in range(table.shape[0])
    ]
    return jnp.concatenate(pieces, axis=0)


def expand(weight_ref, table_ref, taps_last):
    wide = table_ref.shape[-1]
    spread = iota((wide // ROWS, wide), 1) // ROWS == iota((wide // ROWS, wide), 0)
    spread = jnp.where(spread, 1.0, 0.0).astype(bf16)
    if taps_last:
        for o in range(weight_ref.shape[0]):
            table_ref[o] = lax.dot_general(
                weight_ref[o], spread, (((0,), (0,)), ((), ())), preferred_element_type=f32
            )
        return
    for tap in range(weight_ref.shape[0]):
        table_ref[tap] = dot(weight_ref[tap], spread)


def row_bands(width):
    out_row = iota((ROWS, width), 0)
    in_row = lax.rem(iota((ROWS, width), 1), ROWS)
    return [in_row - out_row + 1 == b for b in range(3)]


def banded(table_ref, count, first, step, bands, taps_last):
    pieces = []
    for o in range(count):
        block = jnp.zeros(bands[0].shape, f32)
        for b in range(3):
            tap = first + step * b
            row = table_ref[o, tap : tap + 1, :] if taps_last else table_ref[tap, o : o + 1, :]
            block = jnp.where(bands[b], jnp.broadcast_to(row, block.shape), block)
        pieces.append(block)
    return jnp.concatenate(pieces, axis=0) if count > 1 else pieces[0]


def build_conv(table_ref, count, wide, mat_ref, taps_last):
    bands = row_bands(wide)
    high = count * ROWS
    for a in range(3):
        for e in range(3):
            block = banded(table_ref, count, 9 * a + e, 3, bands, taps_last)
            mat_ref[e * high : (e + 1) * high, a * wide : (a + 1) * wide] = block.astype(
                mat_ref.dtype
            )


def partner(me, depths, k):
    if depths == 4:
        return [me, me + 1 - 2 * lax.rem(me, 2), lax.rem(me + 2, 4), 3 - me][k]
    return lax.rem(me + k, depths)


def origin(me, depths, k):
    return partner(me, depths, k if depths == 4 else (depths - k) % depths)


def feature_stage(
    depths, cols, ready, loaded, run_pass, raw_views, feat_weight, cost_weight, mid_weight, final_weight, frame, own, left,
    right, edge, feats, cost_mat, mid_mat, final_mat, raw, table, cost_table, mid_table, final_table,
    rim, rim_left, rim_right, partial, mat, s_raw, r_raw, s_dep, r_dep, s_right, r_right, s_left, r_left
):
    me, col = lax.axis_index("depth"), lax.axis_index("col")
    count, high, n = raw.shape
    views = depths * count
    channels = high // ROWS
    has_left, has_right = col > 0, col < cols - 1
    first_col = col * n
    lane = iota((high, LANES), 1)
    half = LANES // 2
    raw[...] = raw_views[...].reshape(raw.shape)
    packed = jnp.zeros((high, LANES), bf16)
    for v in range(count):
        first, last = raw[v, :, 0:LANES], raw[v, :, n - LANES : n]
        packed = jnp.where(lane == v, pltpu.roll(first, v, 1) if v else first, packed)
        packed = jnp.where(lane == half + v, pltpu.roll(last, half + v + 1, 1), packed)
    rim[...] = packed
    ready()

    def edge_right():
        return remote(rim, rim_left, s_raw.at[0], r_raw.at[0], me, col + 1)

    def edge_left():
        return remote(rim, rim_right, s_raw.at[1], r_raw.at[1], me, col - 1)

    pl.when(has_right)(lambda: edge_right().start())
    pl.when(has_left)(lambda: edge_left().start())
    loaded()
    expand(feat_weight, table, False)
    bands = row_bands(high)
    for e in range(3):
        mat[e * high : (e + 1) * high, :] = banded(
            table, channels, e, 3, bands, False
        ).astype(bf16)
    column = iota((high, n), 1)
    for v in range(count):
        before = pltpu.roll(dot(mat[0:high, :], raw[v]), 1, 1)
        after = pltpu.roll(dot(mat[2 * high : 3 * high, :], raw[v]), n - 1, 1)
        total = jnp.where(column == 0, 0.0, before) + dot(mat[high : 2 * high, :], raw[v])
        partial[v] = total + jnp.where(column == n - 1, 0.0, after)
    pl.when(has_left)(lambda: edge_right().wait_recv())
    pl.when(has_right)(lambda: edge_left().wait_recv())
    pick = has_left & (lane >= half) & (lane < half + count)
    before = dot(mat[0:high, :], jnp.where(pick, rim_left[...].astype(f32), 0.0).astype(bf16))
    pick = has_right & (lane < count)
    after = dot(
        mat[2 * high : 3 * high, :], jnp.where(pick, rim_right[...].astype(f32), 0.0).astype(bf16)
    )
    zero = jnp.zeros((high, n - LANES), f32)
    for v in range(count):
        low = jnp.where(lane == 0, pltpu.roll(before, half - v, 1), 0.0)
        top = jnp.where(lane == LANES - 1, pltpu.roll(after, LANES - 1 - v, 1), 0.0)
        if n > LANES:
            low = jnp.concatenate([low, zero], axis=1)
            top = jnp.concatenate([zero, top], axis=1)
        own[me * count + v] = (partial[v] + low + top).astype(bf16)

    relayed = depths == 4 and count == 2
    at = [[origin(me, depths, k) * count + j for j in range(count)] for k in range(depths)]
    if relayed:
        groups = [[(0, 0), (0, 1)], [(1, 1), (2, 0)], [(1, 0), (2, 1)], [(3, 0), (3, 1)]]
        direct = [(1, 1), (2, 0), (1, 0), (2, 1)]
        relays = {(1, 1): 2, (2, 0): 1}
    else:
        groups = [[(k, j) for j in range(count)] for k in range(depths)]
        direct = [(k, j) for k in range(1, depths) for j in range(count)]
        relays = {}

    def send(v, k, sem):
        return remote(own.at[v], own.at[v], s_dep.at[sem], r_dep.at[v], partner(me, depths, k), col)

    def relay(k, j):
        return send(at[k][j], relays[k, j], depths * count + relays[k, j])

    def to_depth(k, j):
        return send(me * count + j, k, k * count + j)

    def to_right(v):
        return remote(
            own.at[v, :, n - LANES : n], left.at[v], s_right.at[v], r_right.at[v], me, col + 1
        )

    def to_left():
        return remote(edge, right, s_left.at[0], r_left.at[0], me, col - 1)

    for k, j in direct:
        to_depth(k, j).start()
    for j in range(count):
        pl.when(has_right)(lambda j=j: to_right(me * count + j).start())
    for weight, spread, built, taps_last in (
        (cost_weight, cost_table, cost_mat, False),
        (mid_weight, mid_table, mid_mat, True),
        (final_weight, final_table, final_mat, True),
    ):
        expand(weight, spread, taps_last)
        build_conv(spread, built.shape[0] // (3 * ROWS), built.shape[1] // 3, built, taps_last)

    def absorb(v, source, begin, width):
        c = first_col - LANES + begin + iota((high, width), 1)
        seen = (c >= frame[0, v]) & (c < frame[1, v])
        feats[v, :, begin : begin + width] = jnp.where(seen, source[v], jnp.zeros((high, width), bf16))

    def take(group):
        for k, j in group:
            v = at[k][j]
            if k:
                remote(own.at[v], own.at[v], s_dep.at[0], r_dep.at[v], me, col).wait_recv()
                if (k, j) in relays:
                    relay(k, j).start()
                pl.when(has_right)(lambda v=v: to_right(v).start())
        for k, j in group:
            absorb(at[k][j], own, LANES, n)

    def use(index):
        for k, j in groups[index]:
            v = at[k][j]
            pl.when(has_left)(lambda v=v: to_right(v).wait_recv())
            absorb(v, left, 0, LANES)
        run_pass([at[k][j] for k, j in groups[index]], index == 0, index == len(groups) - 1)

    take(groups[0])
    for index, group in enumerate(groups[1:]):
        take(group)
        if index < len(groups) - 2:
            use(index)
    packed = jnp.zeros((high, LANES), bf16)
    for v in range(views):
        first = own[v, :, 0:LANES]
        packed = jnp.where(lane == v, pltpu.roll(first, v, 1) if v else first, packed)
    edge[...] = packed
    pl.when(has_left)(lambda: to_left().start())
    for index in range(len(groups) - 2, len(groups)):
        use(index)
    pl.when(has_right)(lambda: to_left().wait_recv())

    def finish():
        pl.when(has_right)(lambda: edge_right().wait_send())
        pl.when(has_left)(lambda: edge_left().wait_send())
        for k, j in direct:
            to_depth(k, j).wait_send()
        for k, j in relays:
            relay(k, j).wait_send()
        for v in range(views):
            pl.when(has_right)(lambda v=v: to_right(v).wait_send())
        pl.when(has_left)(lambda: to_left().wait_send())

    return finish


def convolve(slab, wide, mat, halo_left, halo_right, far, high, depth_local, out, pack_left, pack_right,
             stats):
    n = slab.shape[1]
    tiles = n // LANES
    edge_left = edge_right = None
    for a in range(3):
        w_a = mat[0:high, a * wide : (a + 1) * wide]
        w_b = mat[2 * high : 3 * high, a * wide : (a + 1) * wide]
        part_a = pltpu.roll(dot(w_a, halo_left), (LANES - a) % LANES, 1)
        part_b = pltpu.roll(dot(w_b, halo_right), (LANES - a - far) % LANES, 1)
        edge_left = part_a if edge_left is None else edge_left + part_a
        edge_right = part_b if edge_right is None else edge_right + part_b
    lane = iota((high, LANES), 1)
    column = iota((high, n), 1)
    half = depth_local // 2
    weights = mat[...]

    def over_tiles(x):
        return jnp.concatenate([x] * tiles, axis=1) if tiles > 1 else x

    def one_step(t, carry):
        halves = []
        for g in range(2):
            start = pl.multiple_of((t + g * half) * wide, wide)
            halves.append(slab[pl.ds(start, 3 * wide), :])
        product = dot(weights, jnp.concatenate(halves, axis=1))
        carry = list(carry)
        for g in range(2):
            d = t + g * half
            part = product[:, g * n : (g + 1) * n]
            from_left = pltpu.roll(part[0:high], 1, 1)
            from_right = pltpu.roll(part[2 * high : 3 * high], n - 1, 1)
            rim_left = over_tiles(pltpu.roll(edge_left, lax.rem(LANES - d, LANES), 1))
            rim_right = over_tiles(pltpu.roll(edge_right, LANES - 1 - d, 1))
            result = (
                jnp.where(column == 0, rim_left, from_left)
                + part[high : 2 * high]
                + jnp.where(column == n - 1, rim_right, from_right)
            )
            out[d] = result
            if stats is not None:
                carry[0] = carry[0] + result
                carry[1] = carry[1] + result * result
                carry[2] = jnp.where(lane == d, pltpu.roll(result[:, 0:LANES], d, 1), carry[2])
                carry[3] = jnp.where(
                    lane == d, pltpu.roll(result[:, n - LANES : n], d + 1, 1), carry[3]
                )
        return tuple(carry)

    if stats is None:
        lax.fori_loop(0, half, one_step, (), unroll=4)
        return
    wide_zero = jnp.zeros((high, n), f32)
    lane_zero = jnp.zeros((high, LANES), f32)
    first, second, pack_l, pack_r = lax.fori_loop(
        0, half, one_step, (wide_zero, wide_zero, lane_zero, lane_zero), unroll=6
    )
    pack_left[...] = pack_l
    pack_right[...] = pack_r

    def per_channel(x):
        x = sum(x[:, j * LANES : (j + 1) * LANES] for j in range(tiles))
        rows = [
            jnp.sum(x[o * ROWS : (o + 1) * ROWS], axis=0, keepdims=True)
            for o in range(high // ROWS)
        ]
        return jnp.concatenate(rows, axis=0)

    count = high // ROWS
    spot = iota((count, LANES), 1) - iota((count, LANES), 0)
    total = jnp.sum(per_channel(first), axis=1, keepdims=True)
    squares = jnp.sum(per_channel(second), axis=1, keepdims=True)
    row = jnp.where(spot == 0, total, jnp.where(spot == count, squares, 0.0))
    stats[...] = jnp.sum(row, axis=0, keepdims=True)


def volume_pass(
    depth_total, depth_local, picked, first, last, feats, shifts, frame, slab, sum_one, sum_two
):
    views, high, n = feats.shape
    n = n - LANES
    channels = high // ROWS
    first_depth = lax.axis_index("depth") * depth_local
    first_col = lax.axis_index("col") * n
    lane = iota((ROWS, LANES), 1)
    pair_lane = iota((2 * ROWS, LANES), 1)

    def one_depth(step, _):
        depth = first_depth + step - 1
        valid = (depth >= 0) & (depth < depth_total)
        clipped = jnp.clip(depth, 0, depth_total - 1)
        moves = [shifts[v, clipped] for v in picked]
        wraps = [pair_lane >= LANES - move for move in moves]
        for j in range(n // LANES):
            here = slice(j * LANES, (j + 1) * LANES)
            if last:
                x = first_col + j * LANES + lane
                tally = jnp.zeros((ROWS, LANES), f32)
                for v in range(views):
                    c = x - shifts[v, clipped]
                    mask = (c >= frame[0, v]) & (c < frame[1, v])
                    tally = tally + jnp.where(mask, 1.0, 0.0)
                scale = 1.0 / tally
                last_scale = jnp.where(valid, scale, 0.0)
                scale, last_scale = [
                    jnp.concatenate([part, part], axis=0) for part in (scale, last_scale)
                ]
            for pair in range(channels // 2):
                rows = slice(pair * 2 * ROWS, (pair + 1) * 2 * ROWS)
                where_to = pl.ds(pl.multiple_of(step * high + pair * 2 * ROWS, 2 * ROWS), 2 * ROWS)
                ones, twos = [], []
                if not first:
                    ones.append(sum_one[where_to, here])
                    twos.append(sum_two[where_to, here])
                for v, move, wrap in zip(picked, moves, wraps):
                    value = feats[v, rows, (j + 1) * LANES : (j + 2) * LANES]
                    behind = feats[v, rows, here]
                    value = pltpu.roll(jnp.where(wrap, behind, value), move, 1).astype(f32)
                    ones.append(value)
                    twos.append(value * value)
                total, square = tree_sum(ones), tree_sum(twos)
                if last:
                    square = jnp.maximum(square - total * (total * scale), 0.0) * last_scale
                    slab[where_to, here] = square.astype(bf16)
                else:
                    sum_one[where_to, here] = total
                    sum_two[where_to, here] = square
        return _

    lax.fori_loop(0, depth_local + 2, one_depth, 0, unroll=(depth_local + 2) // 2)


def volume_stage(
    depth_total, depth_local, cols, own, left, right, edge, feats, shifts, frame, shift_rows, mat, out,
    pack_left, pack_right, stats, slab, sum_one, sum_two
):
    views, high, n = own.shape
    channels = high // ROWS
    first_depth = lax.axis_index("depth") * depth_local
    first_col = lax.axis_index("col") * n
    view_lane = iota(right.shape, 1)
    ahead = jnp.zeros(right.shape, bf16)
    for v in range(views):
        c = first_col + n
        seen = (c >= frame[0, v]) & (c < frame[1, v]) & (view_lane == v)
        ahead = jnp.where(seen, right[...], ahead)
    half = LANES // 2
    padding = jnp.zeros((views, LANES - depth_total), jnp.int32)
    padded = jnp.concatenate([shift_rows[...], padding], axis=1)
    lane_row = iota((1, LANES), 1)
    far = lane_row >= half
    step_row = jnp.where(far, lane_row - half, lane_row)
    depth_row = first_depth + step_row - 1
    lane_shifts = jnp.where(
        far,
        pltpu.roll(padded, lax.rem(LANES + half + 1 - first_depth, LANES), 1),
        pltpu.roll(padded, lax.rem(LANES + 1 - first_depth, LANES), 1),
    )
    x_row = jnp.where(far, first_col + n, first_col - 1)
    row_id = iota((n + LANES, LANES), 0)
    base = jnp.where(far, n + LANES, LANES - 1)
    total = jnp.zeros((high, LANES), f32)
    squares = jnp.zeros((high, LANES), f32)
    tally = jnp.zeros((1, LANES), f32)
    touch = jnp.zeros((LANES, LANES), f32)
    for v in range(views):
        shift_row = lane_shifts[v : v + 1, :]
        pick = row_id == base - shift_row
        found = dot(feats[v], jnp.where(pick, 1.0, 0.0).astype(bf16))
        total = total + found
        squares = squares + found * found
        c = x_row - shift_row
        tally = tally + jnp.where((c >= frame[0, v]) & (c < frame[1, v]), 1.0, 0.0)
        hit = far & (shift_row == 0) & (iota((LANES, LANES), 0) == v)
        touch = jnp.where(hit, 1.0, touch)
    touch = touch.astype(bf16)
    wide = ahead.astype(f32) * ahead.astype(f32)
    coarse = wide.astype(bf16)
    fine = (wide - coarse.astype(f32)).astype(bf16)
    total = total + dot(ahead, touch)
    squares = squares + dot(coarse, touch) + dot(fine, touch)
    scale = 1.0 / jnp.maximum(tally, 1.0)
    keep = (depth_row >= 0) & (depth_row < depth_total) & (step_row < depth_local + 2)
    keep = keep & (x_row >= 0) & (x_row < n * cols)
    square = jnp.maximum(squares - total * (total * scale), 0.0)
    halo = jnp.where(keep, square * scale, 0.0).astype(bf16)
    convolve(
        slab, high, mat, halo, halo, half, mat.shape[0] // 3, depth_local, out, pack_left, pack_right,
        stats
    )


def exchange(
    depths, cols, voxels, conv, pack_left, pack_right, stats, slab, plane_low, plane_high, from_left,
    from_right, others, s_near, r_near, s_all, r_all, known=None
):
    me, col = lax.axis_index("depth"), lax.axis_index("col")
    depth_local, high, n = conv.shape
    has_left, has_right = col > 0, col < cols - 1
    has_low, has_high = me > 0, me < depths - 1
    def to_all(k):
        kd, kc = k // cols, lax.rem(k, cols)
        return remote(
            stats, others.at[k - 1], s_all.at[0], r_all.at[0], lax.rem(me + kd, depths),
            lax.rem(col + kc, cols)
        )

    if known is not None:
        known()
    if depths * cols > 64:
        lax.fori_loop(1, depths * cols, lambda k, _: (to_all(k).start(), _)[1], 0)
    else:
        for k in range(1, depths * cols):
            to_all(jnp.int32(k)).start()
    near = []
    down = lambda: remote(conv.at[0], plane_high, s_near.at[0], r_near.at[0], me - 1, col)
    up = lambda: remote(
        conv.at[depth_local - 1], plane_low, s_near.at[1], r_near.at[1], me + 1, col
    )
    near.append((down, has_low, has_high))
    near.append((up, has_high, has_low))
    always = col >= 0
    for i, (dd, ok, back) in enumerate(
        ((-1, has_low, has_high), (0, always, always), (1, has_high, has_low))
    ):
        near.append(
            (
                lambda dd=dd, i=i: remote(
                    pack_right, from_left.at[1 - dd], s_near.at[2 + i], r_near.at[2 + i], me + dd, col + 1
                ),
                ok & has_right,
                back & has_left,
            )
        )
        near.append(
            (
                lambda dd=dd, i=i: remote(
                    pack_left, from_right.at[1 - dd], s_near.at[5 + i], r_near.at[5 + i], me + dd, col - 1
                ),
                ok & has_left,
                back & has_right,
            )
        )
    for copy, sends, _ in near:
        pl.when(sends)(lambda copy=copy: copy().start())

    for copy, _, receives in near:
        pl.when(receives)(lambda copy=copy: copy().wait_recv())
    everyone = remote(others, others, s_all.at[0], r_all.at[0], me, col)
    everyone.wait_recv()
    count = high // ROWS
    sums = jnp.broadcast_to(jnp.sum(others[...], axis=0) + stats[...], (count, LANES))
    spot = iota((count, LANES), 1) - iota((count, LANES), 0)

    def pick(at):
        return jnp.sum(jnp.where(spot == at, sums, 0.0), axis=1, keepdims=True) / voxels

    average = pick(0)
    variance = pick(count) - average * average
    average = spread_rows(jnp.broadcast_to(average, (high // ROWS, LANES)))
    factor = spread_rows(jnp.broadcast_to(lax.rsqrt(variance + norm_eps), (high // ROWS, LANES)))

    def activate(x):
        return jnp.maximum((x - average) * factor, 0.0)

    def activate_plane(x):
        parts = [activate(x[:, j * LANES : (j + 1) * LANES]) for j in range(n // LANES)]
        return jnp.concatenate(parts, axis=1) if len(parts) > 1 else parts[0]

    slab[0:high, :] = jnp.where(has_low, activate_plane(plane_low[...]), 0.0).astype(bf16)
    slab[(depth_local + 1) * high : (depth_local + 2) * high, :] = jnp.where(
        has_high, activate_plane(plane_high[...]), 0.0
    ).astype(bf16)

    def one_plane(d, _):
        slab[pl.ds(pl.multiple_of((d + 1) * high, high), high), :] = activate_plane(conv[d]).astype(
            bf16
        )
        return _

    lax.fori_loop(0, depth_local, one_plane, 0, unroll=2)
    lane = iota((high, LANES), 1)
    halos = []
    for parts, ok in ((from_left, has_left), (from_right, has_right)):
        low = pltpu.roll(parts[0], LANES - (depth_local - 1), 1)
        mid = pltpu.roll(parts[1], 1, 1)
        top = pltpu.roll(parts[2], depth_local + 1, 1)
        row = jnp.where(lane == 0, low, jnp.where(lane == depth_local + 1, top, mid))
        keep = ok & (lane <= depth_local + 1)
        keep = keep & (has_low | (lane > 0)) & (has_high | (lane < depth_local + 1))
        halos.append(jnp.where(keep, activate(row), 0.0).astype(bf16))

    def finish():
        everyone.wait_send()
        for copy, sends, _ in near:
            pl.when(sends)(lambda copy=copy: copy().wait_send())

    return halos, finish


def score_stage(
    depths, cols, voxels, depth_total, conv, pack_left, pack_right, stats, mat, out, score, parts,
    s_part, r_part, slab, *rest
):
    me, col = lax.axis_index("depth"), lax.axis_index("col")
    depth_local, high, n = conv.shape
    halos, finish = exchange(
        depths, cols, voxels, conv, pack_left, pack_right, stats, slab, *rest
    )
    convolve(slab, high, mat, halos[0], halos[1], 0, ROWS, depth_local, score, None, None, None)
    planes = [score[d] for d in range(depth_local)]
    peak = functools.reduce(jnp.maximum, planes)
    total = jnp.zeros_like(peak)
    weighted = jnp.zeros_like(peak)
    first_depth = me * depth_local
    for d in range(depth_local):
        term = jnp.exp(planes[d] - peak)
        total = total + term
        weighted = weighted + term * ((first_depth + d).astype(f32) / (depth_total - 1))
    parts[me, 0] = peak
    parts[me, 1] = total
    parts[me, 2] = weighted

    def to_depth(k, slot):
        return remote(
            parts.at[slot], parts.at[slot], s_part.at[k], r_part.at[slot], lax.rem(me + k, depths), col
        )

    for k in range(1, depths):
        to_depth(k, me).start()
    for k in range(1, depths):
        to_depth(k, lax.rem(me + k, depths)).wait_recv()
    highest = functools.reduce(jnp.maximum, [parts[p, 0] for p in range(depths)])
    total = jnp.zeros_like(highest)
    weighted = jnp.zeros_like(highest)
    for p in range(depths):
        scale = jnp.exp(parts[p, 0] - highest)
        total = total + parts[p, 1] * scale
        weighted = weighted + parts[p, 2] * scale
    out[...] = weighted / total
    finish()
    for k in range(1, depths):
        to_depth(k, me).wait_send()


def whole_kernel(groups, depths, cols, voxels, depth_total, depth_local, *refs):
    sources, out = refs[:7], refs[7]
    rest, taken = [], 8
    for size in groups:
        rest.append(refs[taken : taken + size])
        taken += size
    (
        gathered, mats, feature_refs, volume_refs, first, second, swap_a, swap_b, score_refs, known,
        staged
    ) = rest
    known_sem = known[0]
    *targets, shift_rows, s_in = staged
    raw_views, feat_weight, cost_weight, mid_weight, final_weight, shifts, frame = targets
    pairs = list(zip(sources, targets)) + [(sources[5], shift_rows)]
    loads = [
        pltpu.make_async_copy(source, target, s_in.at[i])
        for i, (source, target) in enumerate(pairs)
    ]
    for load in loads:
        load.start()
    me, col = lax.axis_index("depth"), lax.axis_index("col")
    has_left, has_right = col > 0, col < cols - 1
    has_low, has_high = me > 0, me < depths - 1
    count = lambda flag: flag.astype(jnp.int32)
    barrier = pltpu.get_barrier_semaphore()

    def greet(d, c):
        pl.semaphore_signal(barrier, inc=1, device_id=(d, c), device_id_type=MESH)

    for k in range(1, depths):
        greet(lax.rem(me + k, depths), col)
    for k in range(1, cols):
        greet(me, lax.rem(col + k, cols))
    for dd, ok_d in ((-1, has_low), (1, has_high)):
        for dc, ok_c in ((-1, has_left), (1, has_right)):
            pl.when(ok_d & ok_c)(lambda dd=dd, dc=dc: greet(me + dd, col + dc))
    diagonals = (count(has_low) + count(has_high)) * (count(has_left) + count(has_right))

    def ready():
        pl.semaphore_wait(barrier, depths - 1 + cols - 1 + diagonals)
        for k in range(1, cols):
            pl.semaphore_signal(
                known_sem, inc=1, device_id=(me, lax.rem(col + k, cols)), device_id_type=MESH
            )

    def all_known():
        pl.semaphore_wait(known_sem, cols - 1)

    feats = gathered[4]
    loads[0].wait()

    def loaded():
        for load in loads[1:]:
            load.wait()

    def run_pass(picked, first_pass, last_pass):
        volume_pass(
            depth_total, depth_local, picked, first_pass, last_pass, feats, shifts, frame, *volume_refs
        )

    sent = feature_stage(
        depths, cols, ready, loaded, run_pass, raw_views, feat_weight, cost_weight, mid_weight,
        final_weight, frame, *gathered, *mats, *feature_refs
    )
    volume_stage(
        depth_total, depth_local, cols, *gathered, shifts, frame, shift_rows, mats[0], *first,
        *volume_refs
    )
    halos, finish = exchange(depths, cols, voxels, *first, *swap_a, all_known)
    high = first[0].shape[1]
    convolve(swap_a[0], high, mats[1], halos[0], halos[1], 0, high, depth_local, *second)
    finish()
    sent()
    score_stage(depths, cols, voxels, depth_total, *second, mats[2], out, *score_refs, *swap_b)


def buffer(dims, kind):
    return pltpu.VMEM(dims, kind)


def dma(n):
    return pltpu.SemaphoreType.DMA((n,))


def local(raw_views, feat_weight, shifts, frame_range, cost_weight, mid_weight, final_weight):
    view_local, channels, rows, n = raw_views.shape
    depths, cols = lax.axis_size("depth"), lax.axis_size("col")
    views, depth_total = shifts.shape
    depth_local = depth_total // depths
    high = channels * rows
    hidden = cost_weight.shape[1]
    mid_high = hidden * rows
    voxels = float(depth_total * rows * n * cols)

    gathered = [
        buffer((views, high, n), bf16),
        buffer((views, high, LANES), bf16),
        buffer((high, LANES), bf16),
        buffer((high, LANES), bf16),
        buffer((views, high, n + LANES), bf16),
    ]
    mats = [
        buffer((3 * mid_high, 3 * high), bf16),
        buffer((3 * mid_high, 3 * mid_high), bf16),
        buffer((3 * rows, 3 * mid_high), bf16),
    ]
    feature_refs = [
        buffer((view_local, high, n), bf16),
        buffer((9, channels, high), f32),
        buffer((27, hidden, high), f32),
        buffer((hidden, 27, mid_high), f32),
        buffer((1, 27, mid_high), f32),
        buffer((high, LANES), bf16),
        buffer((high, LANES), bf16),
        buffer((high, LANES), bf16),
        buffer((view_local, high, n), f32),
        buffer((3 * high, high), bf16),
        dma(2), dma(2), dma(views + depths), dma(views), dma(views), dma(views), dma(1), dma(1),
    ]
    volume_refs = [
        buffer(((depth_local + 2) * high, n), bf16),
        buffer(((depth_local + 2) * high, n), f32),
        buffer(((depth_local + 2) * high, n), f32),
    ]

    def conv_refs():
        return [
            buffer((depth_local, mid_high, n), f32),
            buffer((mid_high, LANES), f32),
            buffer((mid_high, LANES), f32),
            buffer((1, LANES), f32),
        ]

    def swap_refs():
        return [
            buffer(((depth_local + 2) * mid_high, n), bf16),
            buffer((mid_high, n), f32),
            buffer((mid_high, n), f32),
            buffer((3, mid_high, LANES), f32),
            buffer((3, mid_high, LANES), f32),
            buffer((depths * cols - 1, 1, LANES), f32),
            dma(8), dma(8), dma(1), dma(1),
        ]

    score_refs = [
        buffer((depth_local, rows, n), f32),
        buffer((depths, 3, rows, n), f32),
        dma(depths), dma(depths),
    ]
    operands = [
        raw_views, feat_weight, cost_weight, jnp.transpose(mid_weight, (1, 2, 0)),
        jnp.transpose(final_weight)[None], shifts, jnp.transpose(frame_range)
    ]
    groups = [
        gathered, mats, feature_refs, volume_refs, conv_refs(), conv_refs(), swap_refs(), swap_refs(),
        score_refs, [pltpu.SemaphoreType.REGULAR],
        [buffer(a.shape, a.dtype) for a in operands[:5]]
        + [pltpu.SMEM(a.shape, a.dtype) for a in operands[5:]]
        + [buffer(shifts.shape, jnp.int32), dma(8)],
    ]
    return pl.pallas_call(
        functools.partial(
            whole_kernel, [len(g) for g in groups], depths, cols, voxels, depth_total, depth_local
        ),
        out_shape=jax.ShapeDtypeStruct((rows, n), f32),
        in_specs=[hbm] * 7,
        out_specs=vmem,
        scratch_shapes=[ref for g in groups for ref in g],
        compiler_params=pltpu.CompilerParams(collective_id=0, has_side_effects=True),
        name="whole",
    )(*operands)


def solution(mesh):
    in_specs = (P("depth", None, None, "col"), P(), P(), P(), P(), P(), P())
    out_specs = P(None, "col")
    return jax.shard_map(local, mesh=mesh, in_specs=in_specs, out_specs=out_specs, check_vma=False)
```

```python
import functools
import jax
import jax.numpy as jnp
from jax import lax
from jax.experimental import pallas as pl
from jax.experimental.pallas import tpu as pltpu
from jax.sharding import PartitionSpec as P

norm_eps = 1e-05
LANES = 128
ROWS = 8
f32 = jnp.float32
bf16 = jnp.bfloat16
MESH = pl.DeviceIdType.MESH
vmem = pl.BlockSpec(memory_space=pltpu.VMEM)
hbm = pl.BlockSpec(memory_space=pltpu.HBM)


def dot(a, b):
    return jnp.dot(a, b, preferred_element_type=f32)


def iota(shape, dim):
    return lax.broadcasted_iota(jnp.int32, shape, dim)


def remote(src, dst, send, recv, depth, col):
    return pltpu.make_async_remote_copy(
        src_ref=src,
        dst_ref=dst,
        send_sem=send,
        recv_sem=recv,
        device_id=(depth, col),
        device_id_type=MESH,
    )


def tree_sum(parts):
    while len(parts) > 1:
        paired = [a + b for a, b in zip(parts[::2], parts[1::2])]
        parts = paired + parts[len(paired) * 2 :]
    return parts[0]


def spread_rows(table):
    pieces = [
        jnp.broadcast_to(table[o : o + 1], (ROWS, table.shape[1])) for o in range(table.shape[0])
    ]
    return jnp.concatenate(pieces, axis=0)


def expand(weight_ref, table_ref, taps_last):
    wide = table_ref.shape[-1]
    spread = iota((wide // ROWS, wide), 1) // ROWS == iota((wide // ROWS, wide), 0)
    spread = jnp.where(spread, 1.0, 0.0).astype(bf16)
    if taps_last:
        for o in range(weight_ref.shape[0]):
            table_ref[o] = lax.dot_general(
                weight_ref[o], spread, (((0,), (0,)), ((), ())), preferred_element_type=f32
            )
        return
    for tap in range(weight_ref.shape[0]):
        table_ref[tap] = dot(weight_ref[tap], spread)


def row_bands(width):
    out_row = iota((ROWS, width), 0)
    in_row = lax.rem(iota((ROWS, width), 1), ROWS)
    return [in_row - out_row + 1 == b for b in range(3)]


def banded(table_ref, count, first, step, bands, taps_last):
    pieces = []
    for o in range(count):
        block = jnp.zeros(bands[0].shape, f32)
        for b in range(3):
            tap = first + step * b
            row = table_ref[o, tap : tap + 1, :] if taps_last else table_ref[tap, o : o + 1, :]
            block = jnp.where(bands[b], jnp.broadcast_to(row, block.shape), block)
        pieces.append(block)
    return jnp.concatenate(pieces, axis=0) if count > 1 else pieces[0]


def build_conv(table_ref, count, wide, mat_ref, taps_last):
    bands = row_bands(wide)
    high = count * ROWS
    for a in range(3):
        for e in range(3):
            block = banded(table_ref, count, 9 * a + e, 3, bands, taps_last)
            mat_ref[e * high : (e + 1) * high, a * wide : (a + 1) * wide] = block.astype(
                mat_ref.dtype
            )


def partner(me, depths, k):
    if depths == 4:
        return [me, me + 1 - 2 * lax.rem(me, 2), lax.rem(me + 2, 4), 3 - me][k]
    return lax.rem(me + k, depths)


def origin(me, depths, k):
    return partner(me, depths, k if depths == 4 else (depths - k) % depths)


def feature_stage(
    depths, cols, ready, loaded, prepare, run_pass, raw_views, feat_weight, cost_weight, mid_weight,
    final_weight, frame, own, left,
    right, edge, feats, cost_mat, mid_mat, final_mat, raw, table, cost_table, mid_table, final_table,
    rim, rim_left, rim_right, partial, mat, s_raw, r_raw, s_dep, r_dep, s_right, r_right, s_left, r_left
):
    me, col = lax.axis_index("depth"), lax.axis_index("col")
    count, high, n = raw.shape
    views = depths * count
    channels = high // ROWS
    has_left, has_right = col > 0, col < cols - 1
    first_col = col * n
    lane = iota((high, LANES), 1)
    half = LANES // 2
    raw[...] = raw_views[...].reshape(raw.shape)
    packed = jnp.zeros((high, LANES), bf16)
    for v in range(count):
        first, last = raw[v, :, 0:LANES], raw[v, :, n - LANES : n]
        packed = jnp.where(lane == v, pltpu.roll(first, v, 1) if v else first, packed)
        packed = jnp.where(lane == half + v, pltpu.roll(last, half + v + 1, 1), packed)
    rim[...] = packed
    ready()

    def edge_right():
        return remote(rim, rim_left, s_raw.at[0], r_raw.at[0], me, col + 1)

    def edge_left():
        return remote(rim, rim_right, s_raw.at[1], r_raw.at[1], me, col - 1)

    pl.when(has_right)(lambda: edge_right().start())
    pl.when(has_left)(lambda: edge_left().start())
    loaded()
    expand(feat_weight, table, False)
    bands = row_bands(high)
    for e in range(3):
        mat[e * high : (e + 1) * high, :] = banded(
            table, channels, e, 3, bands, False
        ).astype(bf16)
    column = iota((high, n), 1)
    for v in range(count):
        before = pltpu.roll(dot(mat[0:high, :], raw[v]), 1, 1)
        after = pltpu.roll(dot(mat[2 * high : 3 * high, :], raw[v]), n - 1, 1)
        total = jnp.where(column == 0, 0.0, before) + dot(mat[high : 2 * high, :], raw[v])
        partial[v] = total + jnp.where(column == n - 1, 0.0, after)
    pl.when(has_left)(lambda: edge_right().wait_recv())
    pl.when(has_right)(lambda: edge_left().wait_recv())
    pick = has_left & (lane >= half) & (lane < half + count)
    before = dot(mat[0:high, :], jnp.where(pick, rim_left[...].astype(f32), 0.0).astype(bf16))
    pick = has_right & (lane < count)
    after = dot(
        mat[2 * high : 3 * high, :], jnp.where(pick, rim_right[...].astype(f32), 0.0).astype(bf16)
    )
    zero = jnp.zeros((high, n - LANES), f32)
    for v in range(count):
        low = jnp.where(lane == 0, pltpu.roll(before, half - v, 1), 0.0)
        top = jnp.where(lane == LANES - 1, pltpu.roll(after, LANES - 1 - v, 1), 0.0)
        if n > LANES:
            low = jnp.concatenate([low, zero], axis=1)
            top = jnp.concatenate([zero, top], axis=1)
        own[me * count + v] = (partial[v] + low + top).astype(bf16)

    relayed = depths == 4 and count == 2
    at = [[origin(me, depths, k) * count + j for j in range(count)] for k in range(depths)]
    if relayed:
        groups = [[(0, 0), (0, 1)], [(1, 1), (2, 0)], [(1, 0), (2, 1)], [(3, 0), (3, 1)]]
        direct = [(1, 1), (2, 0), (1, 0), (2, 1)]
        relays = {(1, 1): 2, (2, 0): 1}
    else:
        groups = [[(k, j) for j in range(count)] for k in range(depths)]
        direct = [(k, j) for k in range(1, depths) for j in range(count)]
        relays = {}

    def send(v, k, sem):
        return remote(own.at[v], own.at[v], s_dep.at[sem], r_dep.at[v], partner(me, depths, k), col)

    def relay(k, j):
        return send(at[k][j], relays[k, j], depths * count + relays[k, j])

    def to_depth(k, j):
        return send(me * count + j, k, k * count + j)

    def to_right(v):
        return remote(
            own.at[v, :, n - LANES : n], left.at[v], s_right.at[v], r_right.at[v], me, col + 1
        )

    def to_left():
        return remote(edge, right, s_left.at[0], r_left.at[0], me, col - 1)

    for k, j in direct:
        to_depth(k, j).start()
    for j in range(count):
        pl.when(has_right)(lambda j=j: to_right(me * count + j).start())
    for weight, spread, built, taps_last in (
        (cost_weight, cost_table, cost_mat, False),
        (mid_weight, mid_table, mid_mat, True),
        (final_weight, final_table, final_mat, True),
    ):
        expand(weight, spread, taps_last)
        build_conv(spread, built.shape[0] // (3 * ROWS), built.shape[1] // 3, built, taps_last)

    def absorb(v, source, begin, width):
        c = first_col - LANES + begin + iota((high, width), 1)
        seen = (c >= frame[0, v]) & (c < frame[1, v])
        feats[v, :, begin : begin + width] = jnp.where(seen, source[v], jnp.zeros((high, width), bf16))

    def take(group):
        for k, j in group:
            v = at[k][j]
            if k:
                remote(own.at[v], own.at[v], s_dep.at[0], r_dep.at[v], me, col).wait_recv()
                if (k, j) in relays:
                    relay(k, j).start()
                pl.when(has_right)(lambda v=v: to_right(v).start())
        for k, j in group:
            absorb(at[k][j], own, LANES, n)

    def use(index):
        for k, j in groups[index]:
            v = at[k][j]
            pl.when(has_left)(lambda v=v: to_right(v).wait_recv())
            absorb(v, left, 0, LANES)
        run_pass([at[k][j] for k, j in groups[index]], index == 0, index == len(groups) - 1)

    prepare()
    take(groups[0])
    for index, group in enumerate(groups[1:]):
        take(group)
        if index < len(groups) - 2:
            use(index)
    packed = jnp.zeros((high, LANES), bf16)
    for v in range(views):
        first = own[v, :, 0:LANES]
        packed = jnp.where(lane == v, pltpu.roll(first, v, 1) if v else first, packed)
    edge[...] = packed
    pl.when(has_left)(lambda: to_left().start())
    for index in range(len(groups) - 2, len(groups)):
        use(index)
    pl.when(has_right)(lambda: to_left().wait_recv())

    def finish():
        pl.when(has_right)(lambda: edge_right().wait_send())
        pl.when(has_left)(lambda: edge_left().wait_send())
        for k, j in direct:
            to_depth(k, j).wait_send()
        for k, j in relays:
            relay(k, j).wait_send()
        for v in range(views):
            pl.when(has_right)(lambda v=v: to_right(v).wait_send())
        pl.when(has_left)(lambda: to_left().wait_send())

    return finish


def convolve(slab, wide, mat, halo_left, halo_right, far, high, depth_local, out, pack_left, pack_right,
             stats):
    n = slab.shape[1]
    tiles = n // LANES
    edge_left = edge_right = None
    for a in range(3):
        w_a = mat[0:high, a * wide : (a + 1) * wide]
        w_b = mat[2 * high : 3 * high, a * wide : (a + 1) * wide]
        part_a = pltpu.roll(dot(w_a, halo_left), (LANES - a) % LANES, 1)
        part_b = pltpu.roll(dot(w_b, halo_right), (LANES - a - far) % LANES, 1)
        edge_left = part_a if edge_left is None else edge_left + part_a
        edge_right = part_b if edge_right is None else edge_right + part_b
    lane = iota((high, LANES), 1)
    column = iota((high, n), 1)
    half = depth_local // 2
    weights = mat[...]

    def over_tiles(x):
        return jnp.concatenate([x] * tiles, axis=1) if tiles > 1 else x

    def one_step(t, carry):
        halves = []
        for g in range(2):
            start = pl.multiple_of((t + g * half) * wide, wide)
            halves.append(slab[pl.ds(start, 3 * wide), :])
        product = dot(weights, jnp.concatenate(halves, axis=1))
        carry = list(carry)
        for g in range(2):
            d = t + g * half
            part = product[:, g * n : (g + 1) * n]
            from_left = pltpu.roll(part[0:high], 1, 1)
            from_right = pltpu.roll(part[2 * high : 3 * high], n - 1, 1)
            rim_left = over_tiles(pltpu.roll(edge_left, lax.rem(LANES - d, LANES), 1))
            rim_right = over_tiles(pltpu.roll(edge_right, LANES - 1 - d, 1))
            result = (
                jnp.where(column == 0, rim_left, from_left)
                + part[high : 2 * high]
                + jnp.where(column == n - 1, rim_right, from_right)
            )
            out[d] = result
            if stats is not None:
                carry[0] = carry[0] + result
                carry[1] = carry[1] + result * result
                carry[2] = jnp.where(lane == d, pltpu.roll(result[:, 0:LANES], d, 1), carry[2])
                carry[3] = jnp.where(
                    lane == d, pltpu.roll(result[:, n - LANES : n], d + 1, 1), carry[3]
                )
        return tuple(carry)

    if stats is None:
        lax.fori_loop(0, half, one_step, (), unroll=12)
        return
    wide_zero = jnp.zeros((high, n), f32)
    lane_zero = jnp.zeros((high, LANES), f32)
    first, second, pack_l, pack_r = lax.fori_loop(
        0, half, one_step, (wide_zero, wide_zero, lane_zero, lane_zero), unroll=12
    )
    pack_left[...] = pack_l
    pack_right[...] = pack_r

    def per_channel(x):
        x = sum(x[:, j * LANES : (j + 1) * LANES] for j in range(tiles))
        rows = [
            jnp.sum(x[o * ROWS : (o + 1) * ROWS], axis=0, keepdims=True)
            for o in range(high // ROWS)
        ]
        return jnp.concatenate(rows, axis=0)

    count = high // ROWS
    spot = iota((count, LANES), 1) - iota((count, LANES), 0)
    total = jnp.sum(per_channel(first), axis=1, keepdims=True)
    squares = jnp.sum(per_channel(second), axis=1, keepdims=True)
    row = jnp.where(spot == 0, total, jnp.where(spot == count, squares, 0.0))
    stats[...] = jnp.sum(row, axis=0, keepdims=True)


def count_views(depth_total, depth_local, shifts, frame, scales):
    views = shifts.shape[0]
    n = scales.shape[2]
    first_depth = lax.axis_index("depth") * depth_local
    x = lax.axis_index("col") * n + iota((ROWS, n), 1)

    def one_depth(step, _):
        clipped = jnp.clip(first_depth + step - 1, 0, depth_total - 1)
        tally = jnp.zeros((ROWS, n), f32)
        for v in range(views):
            c = x - shifts[v, clipped]
            tally = tally + jnp.where((c >= frame[0, v]) & (c < frame[1, v]), 1.0, 0.0)
        scales[step] = 1.0 / tally
        return _

    lax.fori_loop(0, depth_local + 2, one_depth, 0, unroll=2)


def volume_pass(
    depth_total, depth_local, picked, first, last, feats, shifts, slab, sum_one, sum_two, scales
):
    views, high, n = feats.shape
    n = n - LANES
    channels = high // ROWS
    first_depth = lax.axis_index("depth") * depth_local
    pair_lane = iota((2 * ROWS, LANES), 1)

    def one_depth(step, _):
        depth = first_depth + step - 1
        valid = (depth >= 0) & (depth < depth_total)
        clipped = jnp.clip(depth, 0, depth_total - 1)
        moves = [shifts[v, clipped] for v in picked]
        wraps = [pair_lane >= LANES - move for move in moves]
        for j in range(n // LANES):
            here = slice(j * LANES, (j + 1) * LANES)
            if last:
                scale = jnp.concatenate([scales[step, :, here]] * 2, axis=0)
                last_scale = jnp.where(valid, scale, 0.0)
            for pair in range(channels // 2):
                rows = slice(pair * 2 * ROWS, (pair + 1) * 2 * ROWS)
                where_to = pl.ds(pl.multiple_of(step * high + pair * 2 * ROWS, 2 * ROWS), 2 * ROWS)
                ones, twos = [], []
                if not first:
                    ones.append(sum_one[where_to, here])
                    twos.append(sum_two[where_to, here])
                for v, move, wrap in zip(picked, moves, wraps):
                    value = feats[v, rows, (j + 1) * LANES : (j + 2) * LANES]
                    behind = feats[v, rows, here]
                    value = pltpu.roll(jnp.where(wrap, behind, value), move, 1).astype(f32)
                    ones.append(value)
                    twos.append(value * value)
                total, square = tree_sum(ones), tree_sum(twos)
                if last:
                    square = jnp.maximum(square - total * (total * scale), 0.0) * last_scale
                    slab[where_to, here] = square.astype(bf16)
                else:
                    sum_one[where_to, here] = total
                    sum_two[where_to, here] = square
        return _

    lax.fori_loop(0, depth_local + 2, one_depth, 0, unroll=(depth_local + 2) // 2)


def volume_stage(
    depth_total, depth_local, cols, own, left, right, edge, feats, shifts, frame, shift_rows, mat, out,
    pack_left, pack_right, stats, slab, sum_one, sum_two, scales
):
    views, high, n = own.shape
    channels = high // ROWS
    first_depth = lax.axis_index("depth") * depth_local
    first_col = lax.axis_index("col") * n
    view_lane = iota(right.shape, 1)
    ahead = jnp.zeros(right.shape, bf16)
    for v in range(views):
        c = first_col + n
        seen = (c >= frame[0, v]) & (c < frame[1, v]) & (view_lane == v)
        ahead = jnp.where(seen, right[...], ahead)
    half = LANES // 2
    padding = jnp.zeros((views, LANES - depth_total), jnp.int32)
    padded = jnp.concatenate([shift_rows[...], padding], axis=1)
    lane_row = iota((1, LANES), 1)
    far = lane_row >= half
    step_row = jnp.where(far, lane_row - half, lane_row)
    depth_row = first_depth + step_row - 1
    lane_shifts = jnp.where(
        far,
        pltpu.roll(padded, lax.rem(LANES + half + 1 - first_depth, LANES), 1),
        pltpu.roll(padded, lax.rem(LANES + 1 - first_depth, LANES), 1),
    )
    x_row = jnp.where(far, first_col + n, first_col - 1)
    row_id = iota((n + LANES, LANES), 0)
    base = jnp.where(far, n + LANES, LANES - 1)
    total = jnp.zeros((high, LANES), f32)
    squares = jnp.zeros((high, LANES), f32)
    tally = jnp.zeros((1, LANES), f32)
    touch = jnp.zeros((LANES, LANES), f32)
    for v in range(views):
        shift_row = lane_shifts[v : v + 1, :]
        pick = row_id == base - shift_row
        found = dot(feats[v], jnp.where(pick, 1.0, 0.0).astype(bf16))
        total = total + found
        squares = squares + found * found
        c = x_row - shift_row
        tally = tally + jnp.where((c >= frame[0, v]) & (c < frame[1, v]), 1.0, 0.0)
        hit = far & (shift_row == 0) & (iota((LANES, LANES), 0) == v)
        touch = jnp.where(hit, 1.0, touch)
    touch = touch.astype(bf16)
    wide = ahead.astype(f32) * ahead.astype(f32)
    coarse = wide.astype(bf16)
    fine = (wide - coarse.astype(f32)).astype(bf16)
    total = total + dot(ahead, touch)
    squares = squares + dot(coarse, touch) + dot(fine, touch)
    scale = 1.0 / jnp.maximum(tally, 1.0)
    keep = (depth_row >= 0) & (depth_row < depth_total) & (step_row < depth_local + 2)
    keep = keep & (x_row >= 0) & (x_row < n * cols)
    square = jnp.maximum(squares - total * (total * scale), 0.0)
    halo = jnp.where(keep, square * scale, 0.0).astype(bf16)
    convolve(
        slab, high, mat, halo, halo, half, mat.shape[0] // 3, depth_local, out, pack_left, pack_right,
        stats
    )


def exchange(
    depths, cols, voxels, conv, pack_left, pack_right, stats, slab, plane_low, plane_high, from_left,
    from_right, others, s_near, r_near, s_all, r_all, known=None
):
    me, col = lax.axis_index("depth"), lax.axis_index("col")
    depth_local, high, n = conv.shape
    has_left, has_right = col > 0, col < cols - 1
    has_low, has_high = me > 0, me < depths - 1
    def to_all(k):
        kd, kc = k // cols, lax.rem(k, cols)
        return remote(
            stats, others.at[k - 1], s_all.at[0], r_all.at[0], lax.rem(me + kd, depths),
            lax.rem(col + kc, cols)
        )

    if known is not None:
        known()
    if depths * cols > 64:
        lax.fori_loop(1, depths * cols, lambda k, _: (to_all(k).start(), _)[1], 0)
    else:
        for k in range(1, depths * cols):
            to_all(jnp.int32(k)).start()
    near = []
    down = lambda: remote(conv.at[0], plane_high, s_near.at[0], r_near.at[0], me - 1, col)
    up = lambda: remote(
        conv.at[depth_local - 1], plane_low, s_near.at[1], r_near.at[1], me + 1, col
    )
    near.append((down, has_low, has_high))
    near.append((up, has_high, has_low))
    always = col >= 0
    for i, (dd, ok, back) in enumerate(
        ((-1, has_low, has_high), (0, always, always), (1, has_high, has_low))
    ):
        near.append(
            (
                lambda dd=dd, i=i: remote(
                    pack_right, from_left.at[1 - dd], s_near.at[2 + i], r_near.at[2 + i], me + dd, col + 1
                ),
                ok & has_right,
                back & has_left,
            )
        )
        near.append(
            (
                lambda dd=dd, i=i: remote(
                    pack_left, from_right.at[1 - dd], s_near.at[5 + i], r_near.at[5 + i], me + dd, col - 1
                ),
                ok & has_left,
                back & has_right,
            )
        )
    for copy, sends, _ in near:
        pl.when(sends)(lambda copy=copy: copy().start())

    for copy, _, receives in near:
        pl.when(receives)(lambda copy=copy: copy().wait_recv())
    everyone = remote(others, others, s_all.at[0], r_all.at[0], me, col)
    everyone.wait_recv()
    count = high // ROWS
    sums = jnp.broadcast_to(jnp.sum(others[...], axis=0) + stats[...], (count, LANES))
    spot = iota((count, LANES), 1) - iota((count, LANES), 0)

    def pick(at):
        return jnp.sum(jnp.where(spot == at, sums, 0.0), axis=1, keepdims=True) / voxels

    average = pick(0)
    variance = pick(count) - average * average
    average = spread_rows(jnp.broadcast_to(average, (high // ROWS, LANES)))
    factor = spread_rows(jnp.broadcast_to(lax.rsqrt(variance + norm_eps), (high // ROWS, LANES)))

    def activate(x):
        return jnp.maximum((x - average) * factor, 0.0)

    def activate_plane(x):
        parts = [activate(x[:, j * LANES : (j + 1) * LANES]) for j in range(n // LANES)]
        return jnp.concatenate(parts, axis=1) if len(parts) > 1 else parts[0]

    slab[0:high, :] = jnp.where(has_low, activate_plane(plane_low[...]), 0.0).astype(bf16)
    slab[(depth_local + 1) * high : (depth_local + 2) * high, :] = jnp.where(
        has_high, activate_plane(plane_high[...]), 0.0
    ).astype(bf16)

    def one_plane(d, _):
        slab[pl.ds(pl.multiple_of((d + 1) * high, high), high), :] = activate_plane(conv[d]).astype(
            bf16
        )
        return _

    lax.fori_loop(0, depth_local, one_plane, 0, unroll=8)
    lane = iota((high, LANES), 1)
    halos = []
    for parts, ok in ((from_left, has_left), (from_right, has_right)):
        low = pltpu.roll(parts[0], LANES - (depth_local - 1), 1)
        mid = pltpu.roll(parts[1], 1, 1)
        top = pltpu.roll(parts[2], depth_local + 1, 1)
        row = jnp.where(lane == 0, low, jnp.where(lane == depth_local + 1, top, mid))
        keep = ok & (lane <= depth_local + 1)
        keep = keep & (has_low | (lane > 0)) & (has_high | (lane < depth_local + 1))
        halos.append(jnp.where(keep, activate(row), 0.0).astype(bf16))

    def finish():
        everyone.wait_send()
        for copy, sends, _ in near:
            pl.when(sends)(lambda copy=copy: copy().wait_send())

    return halos, finish


def score_stage(
    depths, cols, voxels, depth_total, conv, pack_left, pack_right, stats, mat, out, score, parts,
    s_part, r_part, slab, *rest
):
    me, col = lax.axis_index("depth"), lax.axis_index("col")
    depth_local, high, n = conv.shape
    halos, finish = exchange(
        depths, cols, voxels, conv, pack_left, pack_right, stats, slab, *rest
    )
    convolve(slab, high, mat, halos[0], halos[1], 0, ROWS, depth_local, score, None, None, None)
    planes = [score[d] for d in range(depth_local)]
    peak = functools.reduce(jnp.maximum, planes)
    total = jnp.zeros_like(peak)
    weighted = jnp.zeros_like(peak)
    first_depth = me * depth_local
    for d in range(depth_local):
        term = jnp.exp(planes[d] - peak)
        total = total + term
        weighted = weighted + term * ((first_depth + d).astype(f32) / (depth_total - 1))
    parts[me, 0] = peak
    parts[me, 1] = total
    parts[me, 2] = weighted

    def to_depth(k, slot):
        return remote(
            parts.at[slot], parts.at[slot], s_part.at[k], r_part.at[slot], lax.rem(me + k, depths), col
        )

    for k in range(1, depths):
        to_depth(k, me).start()
    for k in range(1, depths):
        to_depth(k, lax.rem(me + k, depths)).wait_recv()
    highest = functools.reduce(jnp.maximum, [parts[p, 0] for p in range(depths)])
    total = jnp.zeros_like(highest)
    weighted = jnp.zeros_like(highest)
    for p in range(depths):
        scale = jnp.exp(parts[p, 0] - highest)
        total = total + parts[p, 1] * scale
        weighted = weighted + parts[p, 2] * scale
    out[...] = weighted / total
    finish()
    for k in range(1, depths):
        to_depth(k, me).wait_send()


def whole_kernel(groups, depths, cols, voxels, depth_total, depth_local, *refs):
    sources, out = refs[:7], refs[7]
    rest, taken = [], 8
    for size in groups:
        rest.append(refs[taken : taken + size])
        taken += size
    (
        gathered, mats, feature_refs, volume_refs, first, second, swap_a, swap_b, score_refs, known,
        staged
    ) = rest
    known_sem = known[0]
    *targets, shift_rows, s_in = staged
    raw_views, feat_weight, cost_weight, mid_weight, final_weight, shifts, frame = targets
    pairs = list(zip(sources, targets)) + [(sources[5], shift_rows)]
    loads = [
        pltpu.make_async_copy(source, target, s_in.at[i])
        for i, (source, target) in enumerate(pairs)
    ]
    for load in loads:
        load.start()
    me, col = lax.axis_index("depth"), lax.axis_index("col")
    has_left, has_right = col > 0, col < cols - 1
    has_low, has_high = me > 0, me < depths - 1
    count = lambda flag: flag.astype(jnp.int32)
    barrier = pltpu.get_barrier_semaphore()

    def greet(d, c):
        pl.semaphore_signal(barrier, inc=1, device_id=(d, c), device_id_type=MESH)

    for k in range(1, depths):
        greet(lax.rem(me + k, depths), col)
    for k in range(1, cols):
        greet(me, lax.rem(col + k, cols))
    for dd, ok_d in ((-1, has_low), (1, has_high)):
        for dc, ok_c in ((-1, has_left), (1, has_right)):
            pl.when(ok_d & ok_c)(lambda dd=dd, dc=dc: greet(me + dd, col + dc))
    diagonals = (count(has_low) + count(has_high)) * (count(has_left) + count(has_right))

    def ready():
        pl.semaphore_wait(barrier, depths - 1 + cols - 1 + diagonals)
        for k in range(1, cols):
            pl.semaphore_signal(
                known_sem, inc=1, device_id=(me, lax.rem(col + k, cols)), device_id_type=MESH
            )

    def all_known():
        pl.semaphore_wait(known_sem, cols - 1)

    feats = gathered[4]
    loads[0].wait()

    def loaded():
        for load in loads[1:]:
            load.wait()

    def prepare():
        count_views(depth_total, depth_local, shifts, frame, volume_refs[3])

    def run_pass(picked, first_pass, last_pass):
        volume_pass(
            depth_total, depth_local, picked, first_pass, last_pass, feats, shifts, *volume_refs
        )

    sent = feature_stage(
        depths, cols, ready, loaded, prepare, run_pass, raw_views, feat_weight, cost_weight, mid_weight,
        final_weight, frame, *gathered, *mats, *feature_refs
    )
    volume_stage(
        depth_total, depth_local, cols, *gathered, shifts, frame, shift_rows, mats[0], *first,
        *volume_refs
    )
    halos, finish = exchange(depths, cols, voxels, *first, *swap_a, all_known)
    high = first[0].shape[1]
    convolve(swap_a[0], high, mats[1], halos[0], halos[1], 0, high, depth_local, *second)
    finish()
    sent()
    score_stage(depths, cols, voxels, depth_total, *second, mats[2], out, *score_refs, *swap_b)


def buffer(dims, kind):
    return pltpu.VMEM(dims, kind)


def dma(n):
    return pltpu.SemaphoreType.DMA((n,))


def local(raw_views, feat_weight, shifts, frame_range, cost_weight, mid_weight, final_weight):
    view_local, channels, rows, n = raw_views.shape
    depths, cols = lax.axis_size("depth"), lax.axis_size("col")
    views, depth_total = shifts.shape
    depth_local = depth_total // depths
    high = channels * rows
    hidden = cost_weight.shape[1]
    mid_high = hidden * rows
    voxels = float(depth_total * rows * n * cols)

    gathered = [
        buffer((views, high, n), bf16),
        buffer((views, high, LANES), bf16),
        buffer((high, LANES), bf16),
        buffer((high, LANES), bf16),
        buffer((views, high, n + LANES), bf16),
    ]
    mats = [
        buffer((3 * mid_high, 3 * high), bf16),
        buffer((3 * mid_high, 3 * mid_high), bf16),
        buffer((3 * rows, 3 * mid_high), bf16),
    ]
    feature_refs = [
        buffer((view_local, high, n), bf16),
        buffer((9, channels, high), f32),
        buffer((27, hidden, high), f32),
        buffer((hidden, 27, mid_high), f32),
        buffer((1, 27, mid_high), f32),
        buffer((high, LANES), bf16),
        buffer((high, LANES), bf16),
        buffer((high, LANES), bf16),
        buffer((view_local, high, n), f32),
        buffer((3 * high, high), bf16),
        dma(2), dma(2), dma(views + depths), dma(views), dma(views), dma(views), dma(1), dma(1),
    ]
    volume_refs = [
        buffer(((depth_local + 2) * high, n), bf16),
        buffer(((depth_local + 2) * high, n), f32),
        buffer(((depth_local + 2) * high, n), f32),
        buffer((depth_local + 2, rows, n), f32),
    ]

    def conv_refs():
        return [
            buffer((depth_local, mid_high, n), f32),
            buffer((mid_high, LANES), f32),
            buffer((mid_high, LANES), f32),
            buffer((1, LANES), f32),
        ]

    def swap_refs():
        return [
            buffer(((depth_local + 2) * mid_high, n), bf16),
            buffer((mid_high, n), f32),
            buffer((mid_high, n), f32),
            buffer((3, mid_high, LANES), f32),
            buffer((3, mid_high, LANES), f32),
            buffer((depths * cols - 1, 1, LANES), f32),
            dma(8), dma(8), dma(1), dma(1),
        ]

    score_refs = [
        buffer((depth_local, rows, n), f32),
        buffer((depths, 3, rows, n), f32),
        dma(depths), dma(depths),
    ]
    operands = [
        raw_views, feat_weight, cost_weight, jnp.transpose(mid_weight, (1, 2, 0)),
        jnp.transpose(final_weight)[None], shifts, jnp.transpose(frame_range)
    ]
    groups = [
        gathered, mats, feature_refs, volume_refs, conv_refs(), conv_refs(), swap_refs(), swap_refs(),
        score_refs, [pltpu.SemaphoreType.REGULAR],
        [buffer(a.shape, a.dtype) for a in operands[:5]]
        + [pltpu.SMEM(a.shape, a.dtype) for a in operands[5:]]
        + [buffer(shifts.shape, jnp.int32), dma(8)],
    ]
    return pl.pallas_call(
        functools.partial(
            whole_kernel, [len(g) for g in groups], depths, cols, voxels, depth_total, depth_local
        ),
        out_shape=jax.ShapeDtypeStruct((rows, n), f32),
        in_specs=[hbm] * 7,
        out_specs=vmem,
        scratch_shapes=[ref for g in groups for ref in g],
        compiler_params=pltpu.CompilerParams(
            collective_id=0, has_side_effects=True, vmem_limit_bytes=40 * 2**20
        ),
        name="whole",
    )(*[pltpu.with_memory_space_constraint(a, pltpu.HBM) for a in operands])


def solution(mesh):
    in_specs = (P("depth", None, None, "col"), P(), P(), P(), P(), P(), P())
    out_specs = P(None, "col")
    return jax.shard_map(local, mesh=mesh, in_specs=in_specs, out_specs=out_specs, check_vma=False)
```
